768 devices in a mesh: sx: 64 (over y, x, core), sy: 12 (over z).
Axes of the slice: x: 4, y: 8, z: 12, core: 2. Of those that a mesh axis runs over, the one named last changes fastest.
Arguments:
- background: bfloat16 [1536, 768, 762], P('sx', 'sy'), may hold values from -6 to 6
- slab_owner: int32 [762], replicated, may hold values from 0 to 767, as said below
- class_length_scale: float32 [16], replicated, may hold values from 0.5 to 16
- band_widths: int32 [16], replicated, may hold values from 1 to 32, as said below
- x_class: int32 [6, 1536], replicated, may hold values from 0 to 15
- y_class: int32 [6, 768], replicated, may hold values from 0 to 15
- z_class: int32 [6, 127], replicated, may hold values from 0 to 15
Outputs:
- filtered_row_energy: float32 [768, 1536], P(('sx', 'sy'))
- covariance_applied: bfloat16 [1536, 768, 762], P('sx', 'sy')
The draws below stay inside these ranges and needn't reach their ends.
Inputs may be any that keep to these rules, and one draw needn't show every extreme that they name: `slab_owner`: each device owns at most 1 slabs, and some device owns exactly 1. `band_widths`: some class has band half-width exactly 32.
All inputs are finite; a program needn't handle non-finite values.
Results may differ from the reference program's by a relative error of at most 0.0076.
Values may be sent and summed in bfloat16 or wider, within the bound.
A program may use at most 64 MiB of HBM per device.

```python
import math
import jax
import jax.numpy as jnp
from jax import lax

NVAR = 6
K = 1
NCLS = 16
LEV = 127
MAXBAND = 32
NX = 1536
NY = 768
SLABS = 762
SLOTS = 768
DEVICES = 768


def draw_slab_owner(key, part):
    order = jax.random.permutation(jax.random.fold_in(key, 11), DEVICES * K).astype(jnp.int32)
    first = order[0]
    partner = first + 1 - 2 * (first % 2)
    where_partner = jnp.argmax(order == partner)
    second = order[1]
    order = order.at[1].set(partner).at[where_partner].set(second)
    return (order[:NVAR * LEV] // K).astype(jnp.int32)


def draw_band_widths(key, part):
    values = jax.random.randint(jax.random.fold_in(key, 5), (NCLS,), 1, MAXBAND + 1)
    chosen = jax.random.randint(jax.random.fold_in(key, 6), (), 0, NCLS)
    return jnp.where(jnp.arange(NCLS) == chosen, MAXBAND, values).astype(jnp.int32)


def with_ends(array, rng, least, top_value):
    extent = array.shape
    spot = [jax.random.randint(jax.random.fold_in(rng, axis), (), 0, extent[axis]) for axis in range(len(extent))]
    array = array.at[tuple(spot)].set(least)
    longest = extent.index(max(extent))
    spot[longest] = (spot[longest] + 1) % extent[longest]
    return array.at[tuple(spot)].set(top_value)


def shard_levels(own_key, extent, pieces, least, top_value):
    def one(axis_at, shards_of):
        heights = jax.random.uniform(jax.random.fold_in(jax.random.fold_in(own_key, 6), axis_at), (shards_of,), jnp.float32, least / len(pieces), top_value / len(pieces))
        return jnp.repeat(jnp.exp(heights), extent[axis_at] // shards_of).reshape((-1,) + (1,) * (len(extent) - axis_at - 1))

    loudness = one(*pieces[0])
    for cut in pieces[1:]:
        loudness = loudness * one(*cut)
    return loudness


def normal_values(own_key, dims, scale, most, shards=(), held_as=jnp.bfloat16):
    drawn = jax.random.normal(own_key, dims, jnp.float32) * scale
    if len(shards) > 0:
        drawn = shard_levels(own_key, dims, shards, -0.22, 0.18) * drawn
    return jnp.clip(drawn, min=-most, max=most).astype(held_as)


def setup_inputs(seed: int = 0) -> dict:
    arg_keys = jax.random.split(jax.random.key(seed), 8)
    background = normal_values(arg_keys[0], (NX, NY, SLABS), 1.0, 6.0, ((0, 64), (1, 12)))
    slab_owner = draw_slab_owner(jax.random.fold_in(arg_keys[7], 71), 0)
    class_length_scale = jnp.clip(jnp.exp(jax.random.uniform(arg_keys[2], (NCLS,), jnp.float32, math.log(0.5), math.log(16.0))), 0.5, 16.0)
    band_widths = draw_band_widths(jax.random.fold_in(arg_keys[7], 71), 0)
    x_class = with_ends(jax.random.randint(arg_keys[4], (NVAR, NX), 0, NCLS), jax.random.fold_in(arg_keys[4], 1), 0, NCLS - 1).astype(jnp.int32)
    y_class = with_ends(jax.random.randint(arg_keys[5], (NVAR, NY), 0, NCLS), jax.random.fold_in(arg_keys[5], 1), 0, NCLS - 1).astype(jnp.int32)
    z_class = with_ends(jax.random.randint(arg_keys[6], (NVAR, LEV), 0, NCLS), jax.random.fold_in(arg_keys[6], 1), 0, NCLS - 1).astype(jnp.int32)
    return {"background": background, "slab_owner": slab_owner, "class_length_scale": class_length_scale, "band_widths": band_widths, "x_class": x_class, "y_class": y_class, "z_class": z_class}


def profile(row_index, col_index, row_class, class_length_scale, band_widths, limit):
    onehot = row_class[..., None] == jnp.arange(class_length_scale.shape[0], dtype=jnp.int32)
    scale = lax.optimization_barrier(jnp.sum(jnp.where(onehot, class_length_scale, jnp.float32(0.0)), -1))
    reach = lax.optimization_barrier(jnp.sum(jnp.where(onehot, band_widths, 0), -1))
    offset = col_index - row_index
    inside = (jnp.abs(offset) <= reach) & (col_index >= 0) & (col_index < limit)
    ratio = offset.astype(jnp.float32) / scale
    return jnp.where(inside, jnp.exp(-0.5 * ratio * ratio), jnp.float32(0.0))

def dense_weights(classes, class_length_scale, band_widths):
    count = classes.shape[0]
    index = jnp.arange(count, dtype=jnp.int32)
    bump = profile(index[:, None], index[None, :], classes[:, None], class_length_scale, band_widths, count)
    return (bump * lax.rsqrt(lax.optimization_barrier(jnp.sum(bump * bump, -1, keepdims=True)))).astype(jnp.bfloat16)

def band_weights(classes, class_length_scale, band_widths, reach):
    count = classes.shape[0]
    index = jnp.arange(count, dtype=jnp.int32)[:, None]
    cols = index + jnp.arange(-reach, reach + 1, dtype=jnp.int32)[None, :]
    bump = profile(index, cols, classes[:, None], class_length_scale, band_widths, count)
    return (bump * lax.rsqrt(lax.optimization_barrier(jnp.sum(bump * bump, -1, keepdims=True)))).astype(jnp.bfloat16)

def reference(background, slab_owner, class_length_scale, band_widths, x_class, y_class, z_class):
    nslab = NVAR * LEV
    x_weights = jax.vmap(lambda c: dense_weights(c, class_length_scale, band_widths))(x_class)
    y_weights = jax.vmap(lambda c: band_weights(c, class_length_scale, band_widths, MAXBAND))(y_class)
    vertical_weight = jax.vmap(lambda c: dense_weights(c, class_length_scale, band_widths))(z_class)

    def one_slab(slab_index):
        control_variable = slab_index // LEV
        piece = lax.dynamic_slice_in_dim(background, slab_index, 1, 2)[:, :, 0]
        x_filtered = jnp.dot(x_weights[control_variable], piece, preferred_element_type=jnp.float32).astype(jnp.bfloat16)
        row_weights = y_weights[control_variable].astype(jnp.float32)
        padded = jnp.pad(x_filtered.astype(jnp.float32), ((0, 0), (MAXBAND, MAXBAND)))

        def add_shift(total, shift):
            shifted = lax.dynamic_slice_in_dim(padded, shift, NY, 1)
            column = lax.dynamic_slice_in_dim(row_weights, shift, 1, 1)[:, 0]
            return (total + shifted * column[None, :], None)
        result, _ = lax.scan(add_shift, jnp.zeros((NX, NY), jnp.float32), jnp.arange(2 * MAXBAND + 1, dtype=jnp.int32))
        return (result.astype(jnp.bfloat16), lax.optimization_barrier(jnp.sum(result * result, 1)))
    y_rounded, energy = lax.map(one_slab, jnp.arange(nslab, dtype=jnp.int32))
    order = jnp.arange(nslab, dtype=jnp.int32)
    same = (slab_owner[:, None] == slab_owner[None, :]) & (order[None, :] < order[:, None])
    rank = lax.optimization_barrier(jnp.sum(same.astype(jnp.int32), 1))
    position = slab_owner * K + rank
    table = jnp.full((SLOTS,), nslab, jnp.int32).at[position].set(order)
    picked = energy[jnp.minimum(table, nslab - 1)]
    filtered_row_energy = jnp.where((table < nslab)[:, None], picked, jnp.float32(0.0))
    column_blocks = y_rounded.reshape(NVAR, LEV, NX * NY)

    def one_variable(control_variable):
        return jnp.dot(vertical_weight[control_variable], column_blocks[control_variable], preferred_element_type=jnp.float32).astype(jnp.bfloat16)
    covariance_result = lax.map(one_variable, jnp.arange(NVAR, dtype=jnp.int32))
    return (filtered_row_energy, covariance_result.reshape(nslab, NX, NY).transpose(1, 2, 0))
```

```python
import functools

import jax
import jax.numpy as jnp
from jax import lax
from jax.experimental import pallas as pl
from jax.experimental.pallas import tpu as pltpu
from jax.sharding import PartitionSpec as P

MESH = pl.DeviceIdType.MESH
REACH = 32
LANES = 128
PACK = 16
F32 = jnp.float32
BF16 = jnp.bfloat16


def iota(shape, dim):
    return lax.broadcasted_iota(jnp.int32, shape, dim)


def lookup(classes, table):
    out = jnp.zeros(classes.shape, table.dtype)
    for k in range(table.shape[0]):
        out = jnp.where(classes == k, table[k], out)
    return out


def bump_of(offset, inside, scale):
    ratio = offset.astype(F32) / scale
    return jnp.where(inside, jnp.exp(-0.5 * ratio * ratio), jnp.float32(0.0))


def normalised(bump):
    return bump * lax.rsqrt(jnp.sum(bump * bump, 0, keepdims=True))


def dot_nt(a, b):
    return lax.dot_general(a, b, (((1,), (1,)), ((), ())), preferred_element_type=F32)


def dot_nn(a, b):
    return jnp.dot(a, b, preferred_element_type=F32)


def split3(value):
    high = value.astype(BF16)
    rest = value - high.astype(F32)
    middle = rest.astype(BF16)
    low = (rest - middle.astype(F32)).astype(BF16)
    return high, middle, low


def kernel(
    size_x,
    size_y,
    lev,
    background,
    scale_table,
    reach_table,
    x_class,
    y_class,
    z_class,
    energy_out,
    cov_out,
    raw,
    win,
    xfw,
    yr,
    kron,
    wy,
    wz,
    wxt,
    spread,
    tables,
    raw_sem,
    near_send,
    near_recv,
    side_send,
    side_recv,
):
    lx, ly, nslab = background.shape
    nvar = z_class.shape[0]
    far = REACH - lx
    span = lx + 2 * REACH
    p = lax.axis_index("sx")
    q = lax.axis_index("sy")
    core = lax.rem(p, 2)

    def at_x(step):
        return (lax.rem(p + step + size_x, size_x), q)

    def at_y(step):
        return (p, lax.rem(q + step + size_y, size_y))

    load = pltpu.make_async_copy(background, raw, raw_sem)
    load.start()
    barrier = pltpu.get_barrier_semaphore()
    for peer in (at_x(-2), at_x(-1), at_x(1), at_x(2), at_y(-1), at_y(1)):
        pl.semaphore_signal(barrier, inc=1, device_id=peer, device_id_type=MESH)

    outer = at_x(2 * core - 1)
    partner = at_x(1 - 2 * core)
    beyond = at_x(2 - 4 * core)

    def remote(src, dst, send, recv, peer):
        return pltpu.make_async_remote_copy(
            src_ref=src, dst_ref=dst, send_sem=send, recv_sem=recv, device_id=peer, device_id_type=MESH
        )

    def to_outer(v):
        own = win.at[v, pl.ds(REACH, lx)]
        return remote(own, win.at[v, pl.ds(REACH + lx - 2 * lx * core, lx)], near_send.at[v, 0], near_recv.at[v, 0], outer)

    def to_partner(v):
        own = win.at[v, pl.ds(REACH, lx)]
        return remote(own, win.at[v, pl.ds(far + 2 * lx * core, lx)], near_send.at[v, 1], near_recv.at[v, 1], partner)

    def to_beyond(v):
        own = win.at[v, pl.ds(REACH + (lx - far) * (1 - core), far)]
        return remote(own, win.at[v, pl.ds((span - far) * core, far)], near_send.at[v, 2], near_recv.at[v, 2], beyond)

    def forward(v):
        got = win.at[v, pl.ds(far + (lx - far) + REACH * core, far)]
        return remote(got, win.at[v, pl.ds((span - far) * core, far)], near_send.at[v, 3], near_recv.at[v, 3], partner)

    def to_left(v):
        own = xfw.at[v, :, pl.ds(REACH, REACH)]
        return remote(own, xfw.at[v, :, pl.ds(REACH + ly, REACH)], side_send.at[v, 0], side_recv.at[v, 0], at_y(-1))

    def to_right(v):
        own = xfw.at[v, :, pl.ds(ly, REACH)]
        return remote(own, xfw.at[v, :, pl.ds(0, REACH)], side_send.at[v, 1], side_recv.at[v, 1], at_y(1))

    def align(v):
        @pl.loop(0, lx)
        def _(i):
            win[v, REACH + i] = jnp.zeros((ly, LANES), BF16)
            win[v, REACH + i, :, 0:lev] = raw[i, :, lev * v : lev * v + lev]

    load.wait()
    align(0)
    pl.semaphore_wait(barrier, 6)
    for v in range(nvar):
        if v + 1 < nvar:
            align(v + 1)
        to_outer(v).start()
        to_beyond(v).start()
        to_partner(v).start()

    n_x = size_x * lx
    n_y = size_y * ly
    lane_x = iota((n_x, LANES), 1)
    pick_x = ((iota((n_x, LANES), 0) == lx * p + lane_x) & (lane_x < lx)).astype(BF16)
    cls_x = (dot_nn(x_class[...].astype(F32).astype(BF16), pick_x) + 0.5).astype(jnp.int32)
    lane_y = iota((n_y, LANES), 1)
    pick_y = ((iota((n_y, LANES), 0) == ly * q + lane_y) & (lane_y < ly)).astype(BF16)
    cls_y = (dot_nn(y_class[...].astype(F32).astype(BF16), pick_y) + 0.5).astype(jnp.int32)
    scale_x, reach_x = lookup(cls_x, scale_table), lookup(cls_x, reach_table)
    scale_y, reach_y = lookup(cls_y, scale_table), lookup(cls_y, reach_table)
    lane = iota((LANES, LANES), 1)
    depth = iota((LANES, LANES), 0)
    offset = depth - REACH - lane
    col_x = lx * p - REACH + depth
    col_y = ly * q - REACH + depth
    eye = (iota((ly, LANES), 0) == iota((ly, LANES), 1)).astype(BF16)
    for v in range(nvar):
        near = jnp.abs(offset)
        inside = (near <= reach_x[v : v + 1]) & (col_x >= 0) & (col_x < n_x) & (depth < span)
        weight = normalised(bump_of(offset, inside, scale_x[v : v + 1]))
        wxt[v] = jnp.where(lane < lx, weight, 0.0).astype(BF16)
        inside = (near <= reach_y[v : v + 1]) & (col_y >= 0) & (col_y < n_y)
        weight = normalised(bump_of(offset, inside, scale_y[v : v + 1]))
        wy[v] = dot_nt(eye, jnp.where(lane < ly, weight, 0.0).astype(BF16)).astype(BF16)

    spread[...] = (iota(spread.shape, 1) // PACK == iota(spread.shape, 0)).astype(BF16)
    part = lx * PACK // 4

    @pl.loop(0, nvar * 4)
    def _(step):
        v = step // 4
        first = pl.multiple_of((step % 4) * part, 16)
        row = iota((part, LANES), 0) + first
        pick = (row // PACK == iota((part, LANES), 1)).astype(BF16)
        rows = dot_nt(pick, wxt[v]).astype(BF16)
        wide = dot_nn(rows, spread[...])
        same = (iota(wide.shape, 0) % PACK) == (iota(wide.shape, 1) % PACK)
        kron[v, pl.ds(first, part), :] = jnp.where(same, wide, 0.0).astype(BF16)

    tables[...] = jnp.zeros(tables.shape, jnp.int32)
    tables[0:nvar, 0:lev] = z_class[...]
    lane1 = iota((8, LANES), 1)
    for t in range(nvar):
        here = pltpu.roll(tables[...], (LANES - t) % LANES, 1)[t : t + 1]
        if t + 1 < nvar:
            there = pltpu.roll(tables[...], lev - t, 1)[t + 1 : t + 2]
        else:
            there = here
        cls_z = jnp.where(lane1[0:1] < lev - t, here, there)
        scale_z, reach_z = lookup(cls_z, scale_table), lookup(cls_z, reach_table)
        own = lane < lev - t
        offset_z = depth - (lane + t)
        inside = (jnp.abs(offset_z) <= reach_z) & own & (depth < lev)
        upper = normalised(bump_of(offset_z, inside, scale_z))
        wz[t, 0:LANES] = jnp.where(own, upper, 0.0).astype(BF16)
        if t + 1 < nvar:
            offset_z = depth - (lane - (lev - t))
            inside = (jnp.abs(offset_z) <= reach_z) & (lane >= lev - t) & (depth < lev)
            lower = normalised(bump_of(offset_z, inside, scale_z))
            wz[t, LANES : 2 * LANES] = jnp.where(lane >= lev - t, lower, 0.0).astype(BF16)

    def filter_x(v):
        @pl.loop(0, ly // (2 * PACK))
        def _(half):
            first = pl.multiple_of(half * 2 * PACK, 2 * PACK)
            left = win[v, :, pl.ds(first, PACK), :].reshape(span * PACK, LANES)
            right = win[v, :, pl.ds(first + PACK, PACK), :].reshape(span * PACK, LANES)
            got = dot_nn(kron[v], jnp.concatenate([left, right], 1)).astype(BF16)
            got = got.reshape(lx, PACK, 2 * LANES)
            xfw[v, :, pl.ds(first + REACH, PACK), :] = got[:, :, 0:LANES]
            xfw[v, :, pl.ds(first + REACH + PACK, PACK), :] = got[:, :, LANES:]

    def filter_y(v):
        @pl.loop(0, lx // 2)
        def _(pair):
            both = jnp.concatenate([xfw[v, 2 * pair], xfw[v, 2 * pair + 1]], 1)
            got = dot_nn(wy[v], both)
            power = jnp.sum(got * got, 0, keepdims=True)
            for k in range(2):
                piece = got[:, LANES * k : LANES * (k + 1)]
                yr[v, 2 * pair + k] = piece.astype(BF16)
                energy_out[v, pl.ds(2 * pair + k, 1), :] = power[:, LANES * k : LANES * (k + 1)]

    def filter_z(t):
        rows = 4
        width = min(LANES, nslab - LANES * t)

        @pl.loop(0, lx // rows)
        def _(block):
            first = block * rows
            here = yr[t, pl.ds(first, rows)].reshape(rows * ly, LANES)
            if t + 1 < nvar:
                there = yr[t + 1, pl.ds(first, rows)].reshape(rows * ly, LANES)
                got = dot_nn(jnp.concatenate([here, there], 1), wz[t])
            else:
                got = dot_nn(here, wz[t, 0:LANES])
            got = got.astype(BF16).reshape(rows, ly, LANES)
            cov_out[pl.ds(first, rows), :, LANES * t : LANES * t + width] = got[:, :, 0:width]

    for v in range(nvar):
        to_outer(v).wait_recv()
        forward(v).start()
        to_beyond(v).wait_recv()
        to_partner(v).wait_recv()
        if v >= 1:
            to_left(v - 1).wait_recv()
            to_right(v - 1).wait_recv()
            filter_y(v - 1)
        if v >= 2:
            filter_z(v - 2)
        forward(v).wait_recv()
        filter_x(v)
        to_left(v).start()
        to_right(v).start()
    v = nvar - 1
    to_left(v).wait_recv()
    to_right(v).wait_recv()
    filter_y(v)
    filter_z(v - 1)
    filter_z(v)

    for v in range(nvar):
        to_outer(v).wait_send()
        to_beyond(v).wait_send()
        to_partner(v).wait_send()
        forward(v).wait_send()
        to_left(v).wait_send()
        to_right(v).wait_send()


def per_device(background, slab_owner, class_length_scale, band_widths, x_class, y_class, z_class):
    lx, ly, nslab = background.shape
    nvar, lev = z_class.shape
    size_x = lax.axis_size("sx")
    size_y = lax.axis_size("sy")
    span = lx + 2 * REACH
    vmem = pl.BlockSpec(memory_space=pltpu.VMEM)
    smem = pl.BlockSpec(memory_space=pltpu.SMEM)
    energy, cov = pl.pallas_call(
        functools.partial(kernel, size_x, size_y, lev),
        out_shape=(
            jax.ShapeDtypeStruct((nvar, lx, LANES), F32),
            jax.ShapeDtypeStruct((lx, ly, nslab), BF16),
        ),
        in_specs=[pl.BlockSpec(memory_space=pl.ANY), smem, smem, vmem, vmem, vmem],
        out_specs=(vmem, vmem),
        scratch_shapes=[
            pltpu.VMEM((lx, ly, nslab), BF16),
            pltpu.VMEM((nvar, span, ly, LANES), BF16),
            pltpu.VMEM((nvar, lx, ly + 2 * REACH, LANES), BF16),
            pltpu.VMEM((nvar, lx, ly, LANES), BF16),
            pltpu.VMEM((nvar, lx * PACK, span * PACK), BF16),
            pltpu.VMEM((nvar, ly, LANES), BF16),
            pltpu.VMEM((nvar, 2 * LANES, LANES), BF16),
            pltpu.VMEM((nvar, LANES, LANES), BF16),
            pltpu.VMEM((LANES, span * PACK), BF16),
            pltpu.VMEM((8, LANES), jnp.int32),
            pltpu.SemaphoreType.DMA,
            pltpu.SemaphoreType.DMA((nvar, 4)),
            pltpu.SemaphoreType.DMA((nvar, 4)),
            pltpu.SemaphoreType.DMA((nvar, 2)),
            pltpu.SemaphoreType.DMA((nvar, 2)),
        ],
        compiler_params=pltpu.CompilerParams(
            collective_id=0, has_side_effects=True, vmem_limit_bytes=60000 * 1024
        ),
    )(background, class_length_scale, band_widths, x_class, y_class, z_class)

    summed = energy[:, :, :lev].transpose(0, 2, 1).reshape(nslab, lx)
    slots = jnp.zeros((size_x * size_y, lx), F32).at[slab_owner].set(summed).reshape(size_x, size_y, lx)
    parts = lax.all_to_all(slots, "sy", split_axis=1, concat_axis=1, tiled=True)
    mine = jnp.sum(parts, 1)
    rows = lax.all_to_all(mine, "sx", split_axis=0, concat_axis=0, tiled=True)
    return rows.reshape(1, size_x * lx), cov


def solution(mesh):
    in_specs = (P("sx", "sy", None), P(), P(), P(), P(), P(), P())
    out_specs = (P(("sx", "sy"), None), P("sx", "sy", None))
    return jax.shard_map(per_device, mesh=mesh, in_specs=in_specs, out_specs=out_specs, check_vma=False)
```

```python
import functools

import jax
import jax.numpy as jnp
from jax import lax
from jax.experimental import pallas as pl
from jax.experimental.pallas import tpu as pltpu
from jax.sharding import PartitionSpec as P

MESH = pl.DeviceIdType.MESH
REACH = 32
LANES = 128
PACK = 8
GROUPS = ((0, 3), (3, 5), (5, 6))
F32 = jnp.float32
BF16 = jnp.bfloat16


def iota(shape, dim):
    return lax.broadcasted_iota(jnp.int32, shape, dim)


def lookup(classes, table):
    out = jnp.zeros(classes.shape, table.dtype)
    for k in range(table.shape[0]):
        out = jnp.where(classes == k, table[k], out)
    return out


def bump_of(offset, inside, scale):
    ratio = offset.astype(F32) / scale
    return jnp.where(inside, jnp.exp(-0.5 * ratio * ratio), jnp.float32(0.0))


def normalised(bump):
    return bump * lax.rsqrt(jnp.sum(bump * bump, 0, keepdims=True))


def dot_nt(a, b):
    return lax.dot_general(a, b, (((1,), (1,)), ((), ())), preferred_element_type=F32)


def dot_nn(a, b):
    return jnp.dot(a, b, preferred_element_type=F32)


def split3(value):
    high = value.astype(BF16)
    rest = value - high.astype(F32)
    middle = rest.astype(BF16)
    low = (rest - middle.astype(F32)).astype(BF16)
    return high, middle, low


def kernel(
    size_x,
    size_y,
    lev,
    background,
    slab_owner,
    scale_table,
    reach_table,
    x_class,
    y_class,
    z_class,
    energy_out,
    cov_out,
    raw,
    win,
    xfw,
    yr,
    kron,
    wy,
    wz,
    wxt,
    spread,
    tables,
    cov,
    onehot,
    mine,
    others,
    rows_out,
    rows_in,
    table,
    fill,
    raw_sem,
    cov_sem,
    near_send,
    near_recv,
    side_send,
    side_recv,
    sum_send,
    sum_recv,
    row_send,
    row_recv,
):
    lx, ly, nslab = background.shape
    nvar = z_class.shape[0]
    far = REACH - lx
    span = lx + 2 * REACH
    p = lax.axis_index("sx")
    q = lax.axis_index("sy")
    core = lax.rem(p, 2)

    def at_x(step):
        return (lax.rem(p + step + size_x, size_x), q)

    def at_y(step):
        return (p, lax.rem(q + step + size_y, size_y))

    load = pltpu.make_async_copy(background, raw, raw_sem)
    load.start()
    barrier = pltpu.get_barrier_semaphore()

    @pl.loop(1, size_y)
    def _(k):
        pl.semaphore_signal(barrier, inc=1, device_id=at_y(k), device_id_type=MESH)

    @pl.loop(1, size_x)
    def _(k):
        pl.semaphore_signal(barrier, inc=1, device_id=at_x(k), device_id_type=MESH)

    outer = at_x(2 * core - 1)
    partner = at_x(1 - 2 * core)
    beyond = at_x(2 - 4 * core)

    def remote(src, dst, send, recv, peer):
        return pltpu.make_async_remote_copy(
            src_ref=src, dst_ref=dst, send_sem=send, recv_sem=recv, device_id=peer, device_id_type=MESH
        )

    def to_outer(v):
        own = win.at[v, :, pl.ds(REACH, lx)]
        return remote(own, win.at[v, :, pl.ds(REACH + lx - 2 * lx * core, lx)], near_send.at[v, 0], near_recv.at[v, 0], outer)

    def to_partner(v):
        own = win.at[v, :, pl.ds(REACH, lx)]
        return remote(own, win.at[v, :, pl.ds(far + 2 * lx * core, lx)], near_send.at[v, 1], near_recv.at[v, 1], partner)

    def to_beyond(v):
        own = win.at[v, :, pl.ds(REACH + (lx - far) * (1 - core), far)]
        return remote(own, win.at[v, :, pl.ds((span - far) * core, far)], near_send.at[v, 2], near_recv.at[v, 2], beyond)

    def forward(v):
        got = win.at[v, :, pl.ds(far + (lx - far) + REACH * core, far)]
        return remote(got, win.at[v, :, pl.ds((span - far) * core, far)], near_send.at[v, 3], near_recv.at[v, 3], partner)

    def to_left(v):
        own = xfw.at[v, :, pl.ds(REACH, REACH)]
        return remote(own, xfw.at[v, :, pl.ds(REACH + ly, REACH)], side_send.at[v, 0], side_recv.at[v, 0], at_y(-1))

    def to_right(v):
        own = xfw.at[v, :, pl.ds(ly, REACH)]
        return remote(own, xfw.at[v, :, pl.ds(0, REACH)], side_send.at[v, 1], side_recv.at[v, 1], at_y(1))

    def align(v):
        rows = 4
        column = iota((ly, LANES), 1)

        @pl.loop(0, lx // rows)
        def _(block):
            for r in range(rows):
                i = block * rows + r
                if LANES * (v + 1) > nslab:
                    win[v, :, REACH + i] = jnp.zeros((ly // PACK, PACK, LANES), BF16)
                    piece = raw[i, :, lev * v : lev * (v + 1)]
                    win[v, :, REACH + i, :, 0:lev] = piece.reshape(ly // PACK, PACK, lev)
                    continue
                tile = raw[i, :, LANES * v : LANES * (v + 1)].astype(F32)
                if v > 0:
                    before = raw[i, :, LANES * (v - 1) : LANES * v].astype(F32)
                    tile = pltpu.roll(jnp.where(column >= LANES - v, before, tile), v, 1)
                tile = jnp.where(column < lev, tile, 0.0).astype(BF16)
                win[v, :, REACH + i] = tile.reshape(ly // PACK, PACK, LANES)

    load.wait()
    align(0)
    pl.semaphore_wait(barrier, size_x + size_y - 2)
    for v in range(nvar):
        if v + 1 < nvar:
            align(v + 1)
        to_outer(v).start()
        to_beyond(v).start()
        to_partner(v).start()

    n_x = size_x * lx
    n_y = size_y * ly
    lane_x = iota((n_x, LANES), 1)
    pick_x = ((iota((n_x, LANES), 0) == lx * p + lane_x) & (lane_x < lx)).astype(BF16)
    cls_x = (dot_nn(x_class[...].astype(F32).astype(BF16), pick_x) + 0.5).astype(jnp.int32)
    lane_y = iota((n_y, LANES), 1)
    pick_y = ((iota((n_y, LANES), 0) == ly * q + lane_y) & (lane_y < ly)).astype(BF16)
    cls_y = (dot_nn(y_class[...].astype(F32).astype(BF16), pick_y) + 0.5).astype(jnp.int32)
    scale_x, reach_x = lookup(cls_x, scale_table), lookup(cls_x, reach_table)
    scale_y, reach_y = lookup(cls_y, scale_table), lookup(cls_y, reach_table)
    lane = iota((LANES, LANES), 1)
    depth = iota((LANES, LANES), 0)
    offset = depth - REACH - lane
    col_x = lx * p - REACH + depth
    col_y = ly * q - REACH + depth
    eye = (iota((ly, LANES), 0) == iota((ly, LANES), 1)).astype(BF16)
    for v in range(nvar):
        near = jnp.abs(offset)
        inside = (near <= reach_x[v : v + 1]) & (col_x >= 0) & (col_x < n_x) & (depth < span)
        weight = normalised(bump_of(offset, inside, scale_x[v : v + 1]))
        wxt[v] = jnp.where(lane < lx, weight, 0.0).astype(BF16)
        inside = (near <= reach_y[v : v + 1]) & (col_y >= 0) & (col_y < n_y)
        weight = normalised(bump_of(offset, inside, scale_y[v : v + 1]))
        wy[v] = dot_nt(eye, jnp.where(lane < ly, weight, 0.0).astype(BF16)).astype(BF16)

    spread[...] = (iota(spread.shape, 1) // PACK == iota(spread.shape, 0)).astype(BF16)
    part = lx * PACK // 2

    @pl.loop(0, nvar * 2)
    def _(step):
        v = step // 2
        first = pl.multiple_of((step % 2) * part, 16)
        row = iota((part, LANES), 0) + first
        pick = (row // PACK == iota((part, LANES), 1)).astype(BF16)
        rows = dot_nt(pick, wxt[v]).astype(BF16)
        wide = dot_nn(rows, spread[...])
        same = (iota(wide.shape, 0) % PACK) == (iota(wide.shape, 1) % PACK)
        kron[v, pl.ds(first, part), :] = jnp.where(same, wide, 0.0).astype(BF16)

    tables[...] = jnp.zeros(tables.shape, jnp.int32)
    tables[0:nvar, 0:lev] = z_class[...]
    lane1 = iota((8, LANES), 1)
    for t in range(nvar):
        here = pltpu.roll(tables[...], (LANES - t) % LANES, 1)[t : t + 1]
        if t + 1 < nvar:
            there = pltpu.roll(tables[...], lev - t, 1)[t + 1 : t + 2]
        else:
            there = here
        cls_z = jnp.where(lane1[0:1] < lev - t, here, there)
        scale_z, reach_z = lookup(cls_z, scale_table), lookup(cls_z, reach_table)
        own = lane < lev - t
        offset_z = depth - (lane + t)
        inside = (jnp.abs(offset_z) <= reach_z) & own & (depth < lev)
        upper = normalised(bump_of(offset_z, inside, scale_z))
        wz[t, 0:LANES] = jnp.where(own, upper, 0.0).astype(BF16)
        if t + 1 < nvar:
            offset_z = depth - (lane - (lev - t))
            inside = (jnp.abs(offset_z) <= reach_z) & (lane >= lev - t) & (depth < lev)
            lower = normalised(bump_of(offset_z, inside, scale_z))
            wz[t, LANES : 2 * LANES] = jnp.where(lane >= lev - t, lower, 0.0).astype(BF16)

    for v in range(nvar):
        fill[...] = jnp.full(fill.shape, -1, jnp.int32)
        fill[0:1, 0:lev] = slab_owner[:, lev * v : lev * (v + 1)]
        owner = fill[0:1, :]
        owner_x = (owner * ((1 << 19) // size_y + 1)) >> 19
        owner_y = owner - owner_x * size_y
        match = (iota((onehot.shape[1], LANES), 0) == owner_x) & (owner_y == q) & (owner >= 0)
        onehot[v] = match.astype(BF16)
    n_out = size_x * lx
    table[...] = (iota(table.shape, 1) % lx == iota(table.shape, 0)).astype(BF16)

    def filter_x(v):
        wide = 4

        @pl.loop(0, ly // (wide * PACK))
        def _(part):
            blocks = [win[v, wide * part + k].reshape(span * PACK, LANES) for k in range(wide)]
            got = dot_nn(kron[v], jnp.concatenate(blocks, 1)).reshape(lx, PACK, wide * LANES)
            for k in range(wide):
                first = pl.multiple_of((wide * part + k) * PACK + REACH, PACK)
                xfw[v, :, pl.ds(first, PACK), :] = got[:, :, LANES * k : LANES * (k + 1)].astype(BF16)

    def filter_y(v):
        rows = 12

        @pl.loop(0, lx // rows)
        def _(block):
            for r in range(0, rows, 2):
                i = block * rows + r
                both = jnp.concatenate([xfw[v, i], xfw[v, i + 1]], 1)
                got = dot_nn(wy[v], both)
                power = jnp.sum(got * got, 0, keepdims=True)
                for k in range(2):
                    yr[v, i + k] = got[:, LANES * k : LANES * (k + 1)].astype(BF16)
                    mine[v, pl.ds(i + k, 1), :] = power[:, LANES * k : LANES * (k + 1)]

    def filter_z(t):
        rows = 8
        width = min(LANES, nslab - LANES * t)

        @pl.loop(0, lx // rows)
        def _(block):
            first = block * rows
            here = yr[t, pl.ds(first, rows)].reshape(rows * ly, LANES)
            if t + 1 < nvar:
                there = yr[t + 1, pl.ds(first, rows)].reshape(rows * ly, LANES)
                got = dot_nn(jnp.concatenate([here, there], 1), wz[t])
            else:
                got = dot_nn(here, wz[t, 0:LANES])
            got = got.astype(BF16).reshape(rows, ly, LANES)
            cov[pl.ds(first, rows), :, LANES * t : LANES * t + width] = got[:, :, 0:width]

    def tell(g, k):
        part = pl.ds(GROUPS[g][0], GROUPS[g][1] - GROUPS[g][0])
        return remote(mine.at[part], others.at[k, part], sum_send.at[g, k], sum_recv.at[g, k], at_y(k))

    def tell_all(g):
        @pl.loop(1, size_y)
        def _(k):
            tell(g, k).start()

    def hand(k):
        to = lax.rem(p + k, size_x)
        return remote(rows_out.at[to], rows_in.at[p], row_send.at[k], row_recv.at[k], (to, q))

    last_of = {stop - 1: g for g, (_, stop) in enumerate(GROUPS)}
    for v in range(nvar):
        to_outer(v).wait_recv()
        forward(v).start()
        to_beyond(v).wait_recv()
        to_partner(v).wait_recv()
        forward(v).wait_recv()
        filter_x(v)
        to_left(v).start()
        to_right(v).start()
        if v >= 1:
            to_left(v - 1).wait_recv()
            to_right(v - 1).wait_recv()
            filter_y(v - 1)
            if v - 1 in last_of:
                tell_all(last_of[v - 1])
        if v >= 2:
            filter_z(v - 2)
    v = nvar - 1
    to_left(v).wait_recv()
    to_right(v).wait_recv()
    filter_y(v)
    tell_all(last_of[v])
    filter_z(v - 1)
    filter_z(v)
    store = pltpu.make_async_copy(cov, cov_out, cov_sem)
    store.start()

    for g in range(len(GROUPS)):
        @pl.loop(1, size_y)
        def _(k):
            tell(g, k).wait()
    picked = jnp.zeros((onehot.shape[1], lx), F32)
    for v in range(nvar):
        total = mine[v]
        for k in range(1, size_y):
            total = total + others[k, v]
        for piece in split3(total):
            picked = picked + dot_nt(onehot[v], piece)
    fill_rows = picked.reshape(onehot.shape[1], 1, lx)
    rows_out[:, :, 0:lx] = fill_rows
    rows_in[p, :, 0:lx] = rows_out[p, :, 0:lx]

    @pl.loop(1, size_x)
    def _(k):
        hand(k).start()

    @pl.loop(1, size_x)
    def _(k):
        hand(k).wait()
    arrived = rows_in[:, :, 0:lx].reshape(size_x, lx)
    home = (iota((size_x, n_out), 1) >= lx * iota((size_x, n_out), 0)) & (
        iota((size_x, n_out), 1) < lx * iota((size_x, n_out), 0) + lx
    )
    spread_rows = jnp.zeros((size_x, n_out), F32)
    for piece in split3(arrived):
        spread_rows = spread_rows + dot_nn(piece, table[...])
    energy_out[...] = jnp.sum(jnp.where(home, spread_rows, 0.0), 0, keepdims=True)

    store.wait()
    for v in range(nvar):
        to_outer(v).wait_send()
        to_beyond(v).wait_send()
        to_partner(v).wait_send()
        forward(v).wait_send()
        to_left(v).wait_send()
        to_right(v).wait_send()


def per_device(background, slab_owner, class_length_scale, band_widths, x_class, y_class, z_class):
    lx, ly, nslab = background.shape
    nvar, lev = z_class.shape
    size_x = lax.axis_size("sx")
    size_y = lax.axis_size("sy")
    span = lx + 2 * REACH
    vmem = pl.BlockSpec(memory_space=pltpu.VMEM)
    smem = pl.BlockSpec(memory_space=pltpu.SMEM)
    energy, cov = pl.pallas_call(
        functools.partial(kernel, size_x, size_y, lev),
        out_shape=(
            jax.ShapeDtypeStruct((1, size_x * lx), F32),
            jax.ShapeDtypeStruct((lx, ly, nslab), BF16),
        ),
        in_specs=[pl.BlockSpec(memory_space=pl.ANY), vmem, smem, smem, vmem, vmem, vmem],
        out_specs=(vmem, pl.BlockSpec(memory_space=pl.ANY)),
        scratch_shapes=[
            pltpu.VMEM((lx, ly, nslab), BF16),
            pltpu.VMEM((nvar, ly // PACK, span, PACK, LANES), BF16),
            pltpu.VMEM((nvar, lx, ly + 2 * REACH, LANES), BF16),
            pltpu.VMEM((nvar, lx, ly, LANES), BF16),
            pltpu.VMEM((nvar, lx * PACK, span * PACK), BF16),
            pltpu.VMEM((nvar, ly, LANES), BF16),
            pltpu.VMEM((nvar, 2 * LANES, LANES), BF16),
            pltpu.VMEM((nvar, LANES, LANES), BF16),
            pltpu.VMEM((LANES, span * PACK), BF16),
            pltpu.VMEM((8, LANES), jnp.int32),
            pltpu.VMEM((lx, ly, nslab), BF16),
            pltpu.VMEM((nvar, size_x, LANES), BF16),
            pltpu.VMEM((nvar, lx, LANES), F32),
            pltpu.VMEM((size_y, nvar, lx, LANES), F32),
            pltpu.VMEM((size_x, 1, LANES), F32),
            pltpu.VMEM((size_x, 1, LANES), F32),
            pltpu.VMEM((lx, size_x * lx), BF16),
            pltpu.VMEM((8, LANES), jnp.int32),
            pltpu.SemaphoreType.DMA,
            pltpu.SemaphoreType.DMA,
            pltpu.SemaphoreType.DMA((nvar, 4)),
            pltpu.SemaphoreType.DMA((nvar, 4)),
            pltpu.SemaphoreType.DMA((nvar, 2)),
            pltpu.SemaphoreType.DMA((nvar, 2)),
            pltpu.SemaphoreType.DMA((len(GROUPS), size_y)),
            pltpu.SemaphoreType.DMA((len(GROUPS), size_y)),
            pltpu.SemaphoreType.DMA((size_x,)),
            pltpu.SemaphoreType.DMA((size_x,)),
        ],
        compiler_params=pltpu.CompilerParams(
            collective_id=0, has_side_effects=True, vmem_limit_bytes=60000 * 1024
        ),
    )(background, slab_owner.reshape(1, nslab), class_length_scale, band_widths, x_class, y_class, z_class)
    return energy, cov


def solution(mesh):
    in_specs = (P("sx", "sy", None), P(), P(), P(), P(), P(), P())
    out_specs = (P(("sx", "sy"), None), P("sx", "sy", None))
    return jax.shard_map(per_device, mesh=mesh, in_specs=in_specs, out_specs=out_specs, check_vma=False)
```

```python
import functools

import jax
import jax.numpy as jnp
from jax import lax
from jax.experimental import pallas as pl
from jax.experimental.pallas import tpu as pltpu
from jax.sharding import PartitionSpec as P

MESH = pl.DeviceIdType.MESH
REACH = 32
LANES = 128
PACK = 8
HALF = 12
STEP = 16
F32 = jnp.float32
BF16 = jnp.bfloat16


def iota(shape, dim):
    return lax.broadcasted_iota(jnp.int32, shape, dim)


def lookup(classes, table):
    out = jnp.zeros(classes.shape, table.dtype)
    for k in range(table.shape[0]):
        out = jnp.where(classes == k, table[k], out)
    return out


def bump_of(offset, inside, scale):
    ratio = offset.astype(F32) / scale
    return jnp.where(inside, jnp.exp(-0.5 * ratio * ratio), jnp.float32(0.0))


def normalised(bump):
    return bump * lax.rsqrt(jnp.sum(bump * bump, 0, keepdims=True))


def dot_nt(a, b):
    return lax.dot_general(a, b, (((1,), (1,)), ((), ())), preferred_element_type=F32)


def dot_nn(a, b):
    return jnp.dot(a, b, preferred_element_type=F32)


def split3(value):
    high = value.astype(BF16)
    rest = value - high.astype(F32)
    middle = rest.astype(BF16)
    low = (rest - middle.astype(F32)).astype(BF16)
    return high, middle, low


def kernel(
    size_x,
    size_y,
    lev,
    background,
    slab_owner,
    scale_table,
    reach_table,
    x_class,
    y_class,
    z_class,
    energy_out,
    cov_out,
    first_tile,
    raw,
    win,
    xfw,
    yr,
    kron,
    wy,
    wz,
    wxt,
    spread,
    tables,
    onehot,
    mine,
    slots,
    outbox,
    inbox,
    rows_out,
    rows_in,
    table,
    fill,
    first_sem,
    raw_sem,
    near_send,
    near_recv,
    side_send,
    side_recv,
    sum_send,
    sum_recv,
    row_send,
    row_recv,
):
    lx, ly, nslab = background.shape
    nvar = z_class.shape[0]
    far = REACH - lx
    span = lx + 2 * REACH
    p = lax.axis_index("sx")
    q = lax.axis_index("sy")
    core = lax.rem(p, 2)
    unroll_x = 7 if size_x % 7 == 1 else 1

    def at_x(step):
        return (lax.rem(p + step + size_x, size_x), q)

    def at_y(step):
        return (p, lax.rem(q + step + size_y, size_y))

    load_first = pltpu.make_async_copy(background.at[:, :, 0:LANES], first_tile, first_sem)
    load_first.start()
    load = pltpu.make_async_copy(background, raw, raw_sem)
    load.start()
    barrier = pltpu.get_barrier_semaphore()

    @pl.loop(1, size_y, unroll=True)
    def _(k):
        pl.semaphore_signal(barrier, inc=1, device_id=at_y(k), device_id_type=MESH)

    @pl.loop(1, size_x, unroll=unroll_x)
    def _(k):
        pl.semaphore_signal(barrier, inc=1, device_id=at_x(k), device_id_type=MESH)

    outer = at_x(2 * core - 1)
    partner = at_x(1 - 2 * core)
    beyond = at_x(2 - 4 * core)

    def remote(src, dst, send, recv, peer):
        return pltpu.make_async_remote_copy(
            src_ref=src, dst_ref=dst, send_sem=send, recv_sem=recv, device_id=peer, device_id_type=MESH
        )

    def to_outer(v):
        own = win.at[v, :, pl.ds(REACH, lx)]
        return remote(own, win.at[v, :, pl.ds(REACH + lx - 2 * lx * core, lx)], near_send.at[v, 0], near_recv.at[v, 0], outer)

    def to_partner(v):
        own = win.at[v, :, pl.ds(REACH, lx)]
        return remote(own, win.at[v, :, pl.ds(far + 2 * lx * core, lx)], near_send.at[v, 1], near_recv.at[v, 1], partner)

    def to_beyond(v):
        own = win.at[v, :, pl.ds(REACH + (lx - far) * (1 - core), far)]
        return remote(own, win.at[v, :, pl.ds((span - far) * core, far)], near_send.at[v, 2], near_recv.at[v, 2], beyond)

    def forward(v):
        got = win.at[v, :, pl.ds(far + (lx - far) + REACH * core, far)]
        return remote(got, win.at[v, :, pl.ds((span - far) * core, far)], near_send.at[v, 3], near_recv.at[v, 3], partner)

    def to_left(v):
        own = xfw.at[v, :, pl.ds(REACH, REACH)]
        return remote(own, xfw.at[v, :, pl.ds(REACH + ly, REACH)], side_send.at[v, 0], side_recv.at[v, 0], at_y(-1))

    def to_right(v):
        own = xfw.at[v, :, pl.ds(ly, REACH)]
        return remote(own, xfw.at[v, :, pl.ds(0, REACH)], side_send.at[v, 1], side_recv.at[v, 1], at_y(1))

    def align(v):
        rows = 4
        column = iota((ly, LANES), 1)

        @pl.loop(0, lx // rows)
        def _(block):
            for r in range(rows):
                i = block * rows + r
                if LANES * (v + 1) > nslab:
                    win[v, :, REACH + i] = jnp.zeros((ly // PACK, PACK, LANES), BF16)
                    piece = raw[i, :, lev * v : lev * (v + 1)]
                    win[v, :, REACH + i, :, 0:lev] = piece.reshape(ly // PACK, PACK, lev)
                    continue
                tile = (first_tile[i] if v == 0 else raw[i, :, LANES * v : LANES * (v + 1)]).astype(F32)
                if v > 0:
                    before = raw[i, :, LANES * (v - 1) : LANES * v].astype(F32)
                    tile = pltpu.roll(jnp.where(column >= LANES - v, before, tile), v, 1)
                tile = jnp.where(column < lev, tile, 0.0).astype(BF16)
                win[v, :, REACH + i] = tile.reshape(ly // PACK, PACK, LANES)

    load_first.wait()
    align(0)
    pl.semaphore_wait(barrier, size_x + size_y - 2)
    for v in range(nvar):
        to_outer(v).start()
        to_beyond(v).start()
        to_partner(v).start()
        if v == 0:
            load.wait()
            align(1)
        if v + 2 < nvar:
            align(v + 2)

    n_x = size_x * lx
    n_y = size_y * ly
    lane_x = iota((n_x, LANES), 1)
    pick_x = ((iota((n_x, LANES), 0) == lx * p + lane_x) & (lane_x < lx)).astype(BF16)
    cls_x = (dot_nn(x_class[...].astype(F32).astype(BF16), pick_x) + 0.5).astype(jnp.int32)
    lane_y = iota((n_y, LANES), 1)
    pick_y = ((iota((n_y, LANES), 0) == ly * q + lane_y) & (lane_y < ly)).astype(BF16)
    cls_y = (dot_nn(y_class[...].astype(F32).astype(BF16), pick_y) + 0.5).astype(jnp.int32)
    scale_x, reach_x = lookup(cls_x, scale_table), lookup(cls_x, reach_table)
    scale_y, reach_y = lookup(cls_y, scale_table), lookup(cls_y, reach_table)
    lane = iota((LANES, LANES), 1)
    depth = iota((LANES, LANES), 0)
    offset = depth - REACH - lane
    col_x = lx * p - REACH + depth
    col_y = ly * q - REACH + depth
    eye = (iota((ly, LANES), 0) == iota((ly, LANES), 1)).astype(BF16)
    for v in range(nvar):
        near = jnp.abs(offset)
        inside = (near <= reach_x[v : v + 1]) & (col_x >= 0) & (col_x < n_x) & (depth < span)
        weight = normalised(bump_of(offset, inside, scale_x[v : v + 1]))
        wxt[v] = jnp.where(lane < lx, weight, 0.0).astype(BF16)
        inside = (near <= reach_y[v : v + 1]) & (col_y >= 0) & (col_y < n_y)
        weight = normalised(bump_of(offset, inside, scale_y[v : v + 1]))
        wy[v] = dot_nt(eye, jnp.where(lane < ly, weight, 0.0).astype(BF16)).astype(BF16)

    spread[...] = (iota(spread.shape, 1) // PACK == iota(spread.shape, 0)).astype(BF16)
    part = lx * PACK // 2

    @pl.loop(0, nvar * 2)
    def _(step):
        v = step // 2
        first = pl.multiple_of((step % 2) * part, 16)
        row = iota((part, LANES), 0) + first
        pick = (row // PACK == iota((part, LANES), 1)).astype(BF16)
        rows = dot_nt(pick, wxt[v]).astype(BF16)
        wide = dot_nn(rows, spread[...])
        same = (iota(wide.shape, 0) % PACK) == (iota(wide.shape, 1) % PACK)
        kron[v, pl.ds(first, part), :] = jnp.where(same, wide, 0.0).astype(BF16)

    tables[...] = jnp.zeros(tables.shape, jnp.int32)
    tables[0:nvar, 0:lev] = z_class[...]
    lane1 = iota((8, LANES), 1)
    for t in range(nvar):
        here = pltpu.roll(tables[...], (LANES - t) % LANES, 1)[t : t + 1]
        if t + 1 < nvar:
            there = pltpu.roll(tables[...], lev - t, 1)[t + 1 : t + 2]
        else:
            there = here
        cls_z = jnp.where(lane1[0:1] < lev - t, here, there)
        scale_z, reach_z = lookup(cls_z, scale_table), lookup(cls_z, reach_table)
        own = lane < lev - t
        offset_z = depth - (lane + t)
        inside = (jnp.abs(offset_z) <= reach_z) & own & (depth < lev)
        upper = normalised(bump_of(offset_z, inside, scale_z))
        wz[t, 0:LANES] = jnp.where(own, upper, 0.0).astype(BF16)
        if t + 1 < nvar:
            offset_z = depth - (lane - (lev - t))
            inside = (jnp.abs(offset_z) <= reach_z) & (lane >= lev - t) & (depth < lev)
            lower = normalised(bump_of(offset_z, inside, scale_z))
            wz[t, LANES : 2 * LANES] = jnp.where(lane >= lev - t, lower, 0.0).astype(BF16)

    fill[...] = jnp.full(fill.shape, -1, jnp.int32)
    for v in range(nvar):
        fill[v : v + 1, 0:lev] = slab_owner[lev * v : lev * (v + 1)].reshape(1, lev)
    for v in range(nvar):
        owner = fill[v : v + 1, :]
        owner_x = (owner * ((1 << 19) // size_y + 1)) >> 19
        place = jnp.where(owner >= 0, owner_x + LANES * (owner - owner_x * size_y), -1)
        onehot[v] = (iota((size_y * LANES, LANES), 0) == place).astype(BF16)
    n_out = size_x * lx
    cell = iota(table.shape, 1) % lx
    table[...] = (cell + (STEP - HALF) * (cell // HALF) == iota(table.shape, 0)).astype(BF16)
    mine[...] = jnp.zeros(mine.shape, F32)
    rows_out[...] = jnp.zeros(rows_out.shape, F32)
    eye_x = (iota((size_x, LANES), 0) == iota((size_x, LANES), 1)).astype(BF16)

    def filter_x(v):
        wide = 4

        @pl.loop(0, ly // (wide * PACK))
        def _(part):
            blocks = [win[v, wide * part + k].reshape(span * PACK, LANES) for k in range(wide)]
            got = dot_nn(kron[v], jnp.concatenate(blocks, 1)).reshape(lx, PACK, wide * LANES)
            for k in range(wide):
                first = pl.multiple_of((wide * part + k) * PACK + REACH, PACK)
                xfw[v, :, pl.ds(first, PACK), :] = got[:, :, LANES * k : LANES * (k + 1)].astype(BF16)

    def filter_y(v):
        rows = HALF

        @pl.loop(0, lx // rows)
        def _(block):
            for r in range(0, rows, 2):
                i = block * rows + r
                both = jnp.concatenate([xfw[v, i], xfw[v, i + 1]], 1)
                got = dot_nn(wy[v], both)
                power = jnp.sum(got * got, 0, keepdims=True)
                for k in range(2):
                    yr[v, i + k] = got[:, LANES * k : LANES * (k + 1)].astype(BF16)
                    mine[v, pl.ds(block * STEP + r + k, 1), :] = power[:, LANES * k : LANES * (k + 1)]

    def filter_z(t):
        rows = 8
        width = min(LANES, nslab - LANES * t)

        @pl.loop(0, lx // rows)
        def _(block):
            first = block * rows
            here = yr[t, pl.ds(first, rows)].reshape(rows * ly, LANES)
            if t + 1 < nvar:
                there = yr[t + 1, pl.ds(first, rows)].reshape(rows * ly, LANES)
                got = dot_nn(jnp.concatenate([here, there], 1), wz[t])
            else:
                got = dot_nn(here, wz[t, 0:LANES])
            got = got.astype(BF16).reshape(rows, ly, LANES)
            cov_out[pl.ds(first, rows), :, LANES * t : LANES * t + width] = got[:, :, 0:width]

    def gather_slots(v):
        got = dot_nt(jnp.concatenate(split3(mine[v]), 0), onehot[v])
        rows = mine.shape[1]
        got = got[0:rows] + got[rows : 2 * rows] + got[2 * rows :]
        if v == 0:
            slots[...] = got
        else:
            slots[...] += got

    def tell(k):
        to = lax.rem(q + k, size_y)
        return remote(outbox.at[to], inbox.at[k], sum_send.at[k], sum_recv.at[k], (p, to))

    def hand(k):
        to = lax.rem(p + k, size_x)
        return remote(rows_out.at[to], rows_in.at[p], row_send.at[k], row_recv.at[k], (to, q))

    for v in range(nvar):
        to_outer(v).wait_recv()
        forward(v).start()
        to_beyond(v).wait_recv()
        to_partner(v).wait_recv()
        forward(v).wait_recv()
        filter_x(v)
        to_left(v).start()
        to_right(v).start()
        if v >= 1:
            to_left(v - 1).wait_recv()
            to_right(v - 1).wait_recv()
            filter_y(v - 1)
            gather_slots(v - 1)
        if v >= 2:
            filter_z(v - 2)
    v = nvar - 1
    to_left(v).wait_recv()
    to_right(v).wait_recv()
    filter_y(v)
    gather_slots(v)
    for to in range(size_y):
        block = slots[:, LANES * to : LANES * (to + 1)]
        outbox[to] = block[0:STEP] + pltpu.roll(block[STEP : 2 * STEP], LANES // 2, 1)

    @pl.loop(1, size_y, unroll=True)
    def _(k):
        tell(k).start()

    filter_z(v - 1)
    filter_z(v)

    @pl.loop(1, size_y, unroll=True)
    def _(k):
        tell(k).wait()

    total = outbox[q]
    for k in range(1, size_y):
        total = total + inbox[k]
    both = jnp.concatenate([total, pltpu.roll(total, LANES // 2, 1)], 0)
    picked = jnp.zeros((size_x, 2 * STEP), F32)
    for piece in split3(both):
        picked = picked + dot_nt(eye_x, piece)
    rows_out[:, :, 0 : 2 * STEP] = picked.reshape(size_x, 1, 2 * STEP)

    @pl.loop(1, size_x, unroll=unroll_x)
    def _(k):
        hand(k).start()

    rows_in[p] = rows_out[p]

    @pl.loop(1, size_x, unroll=unroll_x)
    def _(k):
        hand(k).wait()

    arrived = rows_in[:, :, 0 : 2 * STEP].reshape(size_x, 2 * STEP)
    column = iota((size_x, n_out), 1)
    start = lx * iota((size_x, n_out), 0)
    home = (column >= start) & (column < start + lx)
    wide_rows = dot_nn(jnp.concatenate(split3(arrived), 0), table[...])
    wide_rows = wide_rows[0:size_x] + wide_rows[size_x : 2 * size_x] + wide_rows[2 * size_x :]
    energy_out[...] = jnp.sum(jnp.where(home, wide_rows, 0.0), 0, keepdims=True)

    for v in range(nvar):
        to_outer(v).wait_send()
        to_beyond(v).wait_send()
        to_partner(v).wait_send()
        forward(v).wait_send()
        to_left(v).wait_send()
        to_right(v).wait_send()


def per_device(background, slab_owner, class_length_scale, band_widths, x_class, y_class, z_class):
    lx, ly, nslab = background.shape
    nvar, lev = z_class.shape
    size_x = lax.axis_size("sx")
    size_y = lax.axis_size("sy")
    span = lx + 2 * REACH
    vmem = pl.BlockSpec(memory_space=pltpu.VMEM)
    smem = pl.BlockSpec(memory_space=pltpu.SMEM)
    energy, cov = pl.pallas_call(
        functools.partial(kernel, size_x, size_y, lev),
        out_shape=(
            pltpu.VMEM((1, size_x * lx), F32),
            pltpu.VMEM((lx, ly, nslab), BF16),
        ),
        in_specs=[pl.BlockSpec(memory_space=pl.ANY), vmem, smem, smem, vmem, vmem, vmem],
        out_specs=(vmem, vmem),
        scratch_shapes=[
            pltpu.VMEM((lx, ly, LANES), BF16),
            pltpu.VMEM((lx, ly, nslab), BF16),
            pltpu.VMEM((nvar, ly // PACK, span, PACK, LANES), BF16),
            pltpu.VMEM((nvar, lx, ly + 2 * REACH, LANES), BF16),
            pltpu.VMEM((nvar, lx, ly, LANES), BF16),
            pltpu.VMEM((nvar, lx * PACK, span * PACK), BF16),
            pltpu.VMEM((nvar, ly, LANES), BF16),
            pltpu.VMEM((nvar, 2 * LANES, LANES), BF16),
            pltpu.VMEM((nvar, LANES, LANES), BF16),
            pltpu.VMEM((LANES, span * PACK), BF16),
            pltpu.VMEM((8, LANES), jnp.int32),
            pltpu.VMEM((nvar, size_y * LANES, LANES), BF16),
            pltpu.VMEM((nvar, 2 * STEP, LANES), F32),
            pltpu.VMEM((2 * STEP, size_y * LANES), F32),
            pltpu.VMEM((size_y, STEP, LANES), F32),
            pltpu.VMEM((size_y, STEP, LANES), F32),
            pltpu.VMEM((size_x, 1, LANES), F32),
            pltpu.VMEM((size_x, 1, LANES), F32),
            pltpu.VMEM((2 * STEP, size_x * lx), BF16),
            pltpu.VMEM((8, LANES), jnp.int32),
            pltpu.SemaphoreType.DMA,
            pltpu.SemaphoreType.DMA,
            pltpu.SemaphoreType.DMA((nvar, 4)),
            pltpu.SemaphoreType.DMA((nvar, 4)),
            pltpu.SemaphoreType.DMA((nvar, 2)),
            pltpu.SemaphoreType.DMA((nvar, 2)),
            pltpu.SemaphoreType.DMA((size_y,)),
            pltpu.SemaphoreType.DMA((size_y,)),
            pltpu.SemaphoreType.DMA((size_x,)),
            pltpu.SemaphoreType.DMA((size_x,)),
        ],
        compiler_params=pltpu.CompilerParams(
            collective_id=0, has_side_effects=True, vmem_limit_bytes=60000 * 1024
        ),
    )(background, slab_owner, class_length_scale, band_widths, x_class, y_class, z_class)
    return energy, cov


def solution(mesh):
    in_specs = (P("sx", "sy", None), P(), P(), P(), P(), P(), P())
    out_specs = (P(("sx", "sy"), None), P("sx", "sy", None))
    return jax.shard_map(per_device, mesh=mesh, in_specs=in_specs, out_specs=out_specs, check_vma=False)
```

```python
import functools

import jax
import jax.numpy as jnp
from jax import lax
from jax.experimental import pallas as pl
from jax.experimental.pallas import tpu as pltpu
from jax.sharding import PartitionSpec as P

MESH = pl.DeviceIdType.MESH
REACH = 32
LANES = 128
PACK = 8
HALF = 12
STEP = 16
TURN = 2
F32 = jnp.float32
BF16 = jnp.bfloat16


def iota(shape, dim):
    return lax.broadcasted_iota(jnp.int32, shape, dim)


def lookup(classes, table):
    out = jnp.zeros(classes.shape, table.dtype)
    for k in range(table.shape[0]):
        out = jnp.where(classes == k, table[k], out)
    return out


def bump_of(offset, inside, scale):
    ratio = offset.astype(F32) / scale
    return jnp.where(inside, jnp.exp(-0.5 * ratio * ratio), jnp.float32(0.0))


def normalised(bump):
    return bump * lax.rsqrt(jnp.sum(bump * bump, 0, keepdims=True))


def dot_nt(a, b):
    return lax.dot_general(a, b, (((1,), (1,)), ((), ())), preferred_element_type=F32)


def dot_nn(a, b):
    return jnp.dot(a, b, preferred_element_type=F32)


def split3(value):
    high = value.astype(BF16)
    rest = value - high.astype(F32)
    middle = rest.astype(BF16)
    low = (rest - middle.astype(F32)).astype(BF16)
    return high, middle, low


def kernel(
    size_x,
    size_y,
    lev,
    background,
    slab_owner_hbm,
    scale_table_hbm,
    reach_table_hbm,
    x_class_hbm,
    y_class_hbm,
    z_class_hbm,
    energy_out,
    cov_out,
    first_tile,
    raw,
    win,
    xfw,
    yr,
    kron,
    wy,
    wz,
    wxt,
    spread,
    tables,
    onehot,
    mine,
    slots,
    outbox,
    inbox,
    rows_out,
    rows_in,
    table,
    fill,
    first_sem,
    raw_sem,
    near_send,
    near_recv,
    side_send,
    side_recv,
    sum_send,
    sum_recv,
    row_send,
    row_recv,
    greeted,
    slab_owner,
    scale_table,
    reach_table,
    x_class,
    y_class,
    z_class,
    small_sem,
):
    lx, ly, nslab = background.shape
    nvar = z_class.shape[0]
    far = REACH - lx
    span = lx + 2 * REACH
    p = lax.axis_index("sx")
    q = lax.axis_index("sy")
    core = lax.rem(p, 2)
    unroll_x = 7 if size_x % 7 == 1 else 1

    def at_x(step):
        return (lax.rem(p + step + size_x, size_x), q)

    def at_y(step):
        return (p, lax.rem(q + step + size_y, size_y))

    load_first = pltpu.make_async_copy(background.at[:, :, 0:LANES], first_tile, first_sem)
    load_first.start()
    load = pltpu.make_async_copy(background, raw, raw_sem)
    load.start()
    smalls = []
    for k, (src, dst) in enumerate((
        (slab_owner_hbm, slab_owner), (scale_table_hbm, scale_table), (reach_table_hbm, reach_table),
        (x_class_hbm, x_class), (y_class_hbm, y_class), (z_class_hbm, z_class),
    )):
        smalls.append(pltpu.make_async_copy(src, dst, small_sem.at[k]))
        smalls[-1].start()
    barrier = pltpu.get_barrier_semaphore()

    near = (at_x(-2), at_x(-1), at_x(1), at_x(2), at_y(-1), at_y(1))
    for peer in near:
        pl.semaphore_signal(barrier, inc=1, device_id=peer, device_id_type=MESH)

    def doublings(known, size):
        reach = []
        while known < size // 2:
            reach.append(known)
            known *= 2
        return reach

    rounds = max(len(doublings(2, size_x)), len(doublings(1, size_y)))

    def greet(r):
        for axis, at, reach in ((0, at_x, doublings(2, size_x)), (1, at_y, doublings(1, size_y))):
            if r < len(reach):
                for side, step in ((0, reach[r]), (1, -reach[r])):
                    pl.semaphore_signal(greeted.at[axis, r, side], inc=1, device_id=at(step), device_id_type=MESH)

    def heard(r):
        for axis, reach in ((0, doublings(2, size_x)), (1, doublings(1, size_y))):
            if r < len(reach):
                for side in range(2):
                    pl.semaphore_wait(greeted.at[axis, r, side], 1)

    outer = at_x(2 * core - 1)
    partner = at_x(1 - 2 * core)
    beyond = at_x(2 - 4 * core)

    def remote(src, dst, send, recv, peer):
        return pltpu.make_async_remote_copy(
            src_ref=src, dst_ref=dst, send_sem=send, recv_sem=recv, device_id=peer, device_id_type=MESH
        )

    blocks = ly // PACK
    cut = blocks // 2
    units = [(v, 0, blocks) for v in range(nvar - 1)] + [(nvar - 1, 0, cut), (nvar - 1, cut, blocks - cut)]

    def window(u, first, count):
        return win.at[units[u][0], pl.ds(units[u][1], units[u][2]), pl.ds(first, count)]

    def to_outer(u):
        own = window(u, REACH, lx)
        return remote(own, window(u, REACH + lx - 2 * lx * core, lx), near_send.at[u, 0], near_recv.at[u, 0], outer)

    def to_partner(u):
        own = window(u, REACH, lx)
        return remote(own, window(u, far + 2 * lx * core, lx), near_send.at[u, 1], near_recv.at[u, 1], partner)

    def to_beyond(u):
        own = window(u, REACH + (lx - far) * (1 - core), far)
        return remote(own, window(u, (span - far) * core, far), near_send.at[u, 2], near_recv.at[u, 2], beyond)

    def forward(u):
        got = window(u, far + (lx - far) + REACH * core, far)
        return remote(got, window(u, (span - far) * core, far), near_send.at[u, 3], near_recv.at[u, 3], partner)

    def columns(u):
        if units[u][2] == blocks:
            return 0, 0, REACH
        return (TURN * PACK, 0, TURN * PACK) if units[u][1] == 0 else (0, TURN * PACK, TURN * PACK)

    def to_left(u):
        v, (first, _, count) = units[u][0], columns(u)
        own = xfw.at[v, :, pl.ds(REACH + first, count)]
        return remote(own, xfw.at[v, :, pl.ds(REACH + ly + first, count)], side_send.at[u, 0], side_recv.at[u, 0], at_y(-1))

    def to_right(u):
        v, (_, first, count) = units[u][0], columns(u)
        own = xfw.at[v, :, pl.ds(ly + first, count)]
        return remote(own, xfw.at[v, :, pl.ds(first, count)], side_send.at[u, 1], side_recv.at[u, 1], at_y(1))

    def align(v):
        rows = 4
        column = iota((ly, LANES), 1)

        @pl.loop(0, lx // rows)
        def _(block):
            for r in range(rows):
                i = block * rows + r
                if LANES * (v + 1) > nslab:
                    win[v, :, REACH + i] = jnp.zeros((ly // PACK, PACK, LANES), BF16)
                    piece = raw[i, :, lev * v : lev * (v + 1)].reshape(blocks, PACK, lev)
                    win[v, 0 : blocks - TURN, REACH + i, :, 0:lev] = piece[TURN:]
                    win[v, blocks - TURN : blocks, REACH + i, :, 0:lev] = piece[:TURN]
                    continue
                tile = (first_tile[i] if v == 0 else raw[i, :, LANES * v : LANES * (v + 1)]).astype(F32)
                if v > 0:
                    before = raw[i, :, LANES * (v - 1) : LANES * v].astype(F32)
                    tile = pltpu.roll(jnp.where(column >= LANES - v, before, tile), v, 1)
                tile = jnp.where(column < lev, tile, 0.0).astype(BF16)
                tile = tile.reshape(blocks, PACK, LANES)
                win[v, 0 : blocks - TURN, REACH + i] = tile[TURN:]
                win[v, blocks - TURN : blocks, REACH + i] = tile[:TURN]

    load_first.wait()
    align(0)
    pl.semaphore_wait(barrier, len(near))
    for u in range(len(units)):
        to_outer(u).start()
        to_beyond(u).start()
        to_partner(u).start()
        if u == 0:
            greet(0)
            load.wait()
            align(1)
        if u + 2 < nvar:
            align(u + 2)
    for copy in smalls:
        copy.wait()

    n_x = size_x * lx
    n_y = size_y * ly
    lane_x = iota((n_x, LANES), 1)
    pick_x = ((iota((n_x, LANES), 0) == lx * p + lane_x) & (lane_x < lx)).astype(BF16)
    cls_x = (dot_nn(x_class[...].astype(F32).astype(BF16), pick_x) + 0.5).astype(jnp.int32)
    lane_y = iota((n_y, LANES), 1)
    pick_y = ((iota((n_y, LANES), 0) == ly * q + lane_y) & (lane_y < ly)).astype(BF16)
    cls_y = (dot_nn(y_class[...].astype(F32).astype(BF16), pick_y) + 0.5).astype(jnp.int32)
    scale_x, reach_x = lookup(cls_x, scale_table), lookup(cls_x, reach_table)
    scale_y, reach_y = lookup(cls_y, scale_table), lookup(cls_y, reach_table)
    lane = iota((LANES, LANES), 1)
    depth = iota((LANES, LANES), 0)
    offset = depth - REACH - lane
    col_x = lx * p - REACH + depth
    col_y = ly * q - REACH + depth
    eye = (iota((ly, LANES), 0) == iota((ly, LANES), 1)).astype(BF16)
    for v in range(nvar):
        near = jnp.abs(offset)
        inside = (near <= reach_x[v : v + 1]) & (col_x >= 0) & (col_x < n_x) & (depth < span)
        weight = normalised(bump_of(offset, inside, scale_x[v : v + 1]))
        wxt[v] = jnp.where(lane < lx, weight, 0.0).astype(BF16)
        inside = (near <= reach_y[v : v + 1]) & (col_y >= 0) & (col_y < n_y)
        weight = normalised(bump_of(offset, inside, scale_y[v : v + 1]))
        wy[v] = dot_nt(eye, jnp.where(lane < ly, weight, 0.0).astype(BF16)).astype(BF16)

    spread[...] = (iota(spread.shape, 1) // PACK == iota(spread.shape, 0)).astype(BF16)
    part = lx * PACK // 2

    @pl.loop(0, nvar * 2)
    def _(step):
        v = step // 2
        first = pl.multiple_of((step % 2) * part, 16)
        row = iota((part, LANES), 0) + first
        pick = (row // PACK == iota((part, LANES), 1)).astype(BF16)
        rows = dot_nt(pick, wxt[v]).astype(BF16)
        wide = dot_nn(rows, spread[...])
        same = (iota(wide.shape, 0) % PACK) == (iota(wide.shape, 1) % PACK)
        kron[v, pl.ds(first, part), :] = jnp.where(same, wide, 0.0).astype(BF16)

    tables[...] = jnp.zeros(tables.shape, jnp.int32)
    tables[0:nvar, 0:lev] = z_class[...]
    lane1 = iota((8, LANES), 1)
    for t in range(nvar):
        here = pltpu.roll(tables[...], (LANES - t) % LANES, 1)[t : t + 1]
        if t + 1 < nvar:
            there = pltpu.roll(tables[...], lev - t, 1)[t + 1 : t + 2]
        else:
            there = here
        cls_z = jnp.where(lane1[0:1] < lev - t, here, there)
        scale_z, reach_z = lookup(cls_z, scale_table), lookup(cls_z, reach_table)
        own = lane < lev - t
        offset_z = depth - (lane + t)
        inside = (jnp.abs(offset_z) <= reach_z) & own & (depth < lev)
        upper = normalised(bump_of(offset_z, inside, scale_z))
        wz[t, 0:LANES] = jnp.where(own, upper, 0.0).astype(BF16)
        if t + 1 < nvar:
            offset_z = depth - (lane - (lev - t))
            inside = (jnp.abs(offset_z) <= reach_z) & (lane >= lev - t) & (depth < lev)
            lower = normalised(bump_of(offset_z, inside, scale_z))
            wz[t, LANES : 2 * LANES] = jnp.where(lane >= lev - t, lower, 0.0).astype(BF16)

    fill[...] = jnp.full(fill.shape, -1, jnp.int32)
    for v in range(nvar):
        fill[v : v + 1, 0:lev] = slab_owner[lev * v : lev * (v + 1)].reshape(1, lev)
    for v in range(nvar):
        owner = fill[v : v + 1, :]
        owner_x = (owner * ((1 << 19) // size_y + 1)) >> 19
        place = jnp.where(owner >= 0, owner_x + LANES * (owner - owner_x * size_y), -1)
        onehot[v] = (iota((size_y * LANES, LANES), 0) == place).astype(BF16)
    n_out = size_x * lx
    cell = iota(table.shape, 1) % lx
    table[...] = (cell + (STEP - HALF) * (cell // HALF) == iota(table.shape, 0)).astype(BF16)
    mine[...] = jnp.zeros(mine.shape, F32)
    rows_out[...] = jnp.zeros(rows_out.shape, F32)
    eye_x = (iota((size_x, LANES), 0) == iota((size_x, LANES), 1)).astype(BF16)

    def filter_x(u):
        v, first_block, count = units[u]
        wide = 4

        def some(at):
            parts = [win[v, at + k].reshape(span * PACK, LANES) for k in range(wide)]
            got = dot_nn(kron[v], jnp.concatenate(parts, 1)).reshape(lx, PACK, wide * LANES)
            for k in range(wide):
                first = lax.rem(at + k + TURN, blocks) * PACK + REACH
                first = first if isinstance(first, int) else pl.multiple_of(first, PACK)
                xfw[v, :, pl.ds(first, PACK), :] = got[:, :, LANES * k : LANES * (k + 1)].astype(BF16)

        if count == wide:
            some(jnp.int32(first_block))
        else:

            @pl.loop(0, count // wide)
            def _(step):
                some(wide * step)

    def filter_y(v):
        rows = HALF

        @pl.loop(0, lx // rows)
        def _(block):
            for r in range(0, rows, 2):
                i = block * rows + r
                both = jnp.concatenate([xfw[v, i], xfw[v, i + 1]], 1)
                got = dot_nn(wy[v], both)
                power = jnp.sum(got * got, 0, keepdims=True)
                for k in range(2):
                    yr[v, i + k] = got[:, LANES * k : LANES * (k + 1)].astype(BF16)
                    mine[v, pl.ds(block * STEP + r + k, 1), :] = power[:, LANES * k : LANES * (k + 1)]

    def filter_z(t):
        rows = 8
        width = min(LANES, nslab - LANES * t)

        @pl.loop(0, lx // rows)
        def _(block):
            first = block * rows
            here = yr[t, pl.ds(first, rows)].reshape(rows * ly, LANES)
            if t + 1 < nvar:
                there = yr[t + 1, pl.ds(first, rows)].reshape(rows * ly, LANES)
                got = dot_nn(jnp.concatenate([here, there], 1), wz[t])
            else:
                got = dot_nn(here, wz[t, 0:LANES])
            got = got.astype(BF16).reshape(rows, ly, LANES)
            cov_out[pl.ds(first, rows), :, LANES * t : LANES * t + width] = got[:, :, 0:width]

    def gather_slots(v):
        got = dot_nt(jnp.concatenate(split3(mine[v]), 0), onehot[v])
        rows = mine.shape[1]
        got = got[0:rows] + got[rows : 2 * rows] + got[2 * rows :]
        if v == 0:
            slots[...] = got
        else:
            slots[...] += got

    def tell(k):
        to = lax.rem(q + k, size_y)
        return remote(outbox.at[to], inbox.at[k], sum_send.at[k], sum_recv.at[k], (p, to))

    def hand(k):
        to = lax.rem(p + k, size_x)
        return remote(rows_out.at[to], rows_in.at[p], row_send.at[k], row_recv.at[k], (to, q))

    def arrive(u):
        to_outer(u).wait_recv()
        forward(u).start()
        to_beyond(u).wait_recv()
        to_partner(u).wait_recv()
        forward(u).wait_recv()
        filter_x(u)
        to_left(u).start()
        to_right(u).start()

    def sides(v):
        for u in range(len(units)):
            if units[u][0] == v:
                to_left(u).wait_recv()
                to_right(u).wait_recv()

    heard(0)
    greet(1)
    for u in range(nvar):
        arrive(u)
        if u + 1 < rounds:
            heard(u + 1)
            greet(u + 2)
        if u >= 1:
            sides(u - 1)
            filter_y(u - 1)
            gather_slots(u - 1)
        if 2 <= u < nvar - 1:
            filter_z(u - 2)
    v = nvar - 1
    arrive(nvar)
    filter_z(v - 2)
    sides(v)
    filter_y(v)
    gather_slots(v)
    for to in range(size_y):
        block = slots[:, LANES * to : LANES * (to + 1)]
        outbox[to] = block[0:STEP] + pltpu.roll(block[STEP : 2 * STEP], LANES // 2, 1)

    for k in sorted(range(1, size_y), key=lambda k: abs(2 * k - size_y)):
        tell(k).start()

    filter_z(v - 1)
    filter_z(v)

    @pl.loop(1, size_y, unroll=True)
    def _(k):
        tell(k).wait()

    total = outbox[q]
    for k in range(1, size_y):
        total = total + inbox[k]
    both = jnp.concatenate([total, pltpu.roll(total, LANES // 2, 1)], 0)
    picked = jnp.zeros((size_x, 2 * STEP), F32)
    for piece in split3(both):
        picked = picked + dot_nt(eye_x, piece)
    rows_out[:, :, 0 : 2 * STEP] = picked.reshape(size_x, 1, 2 * STEP)

    middle = size_x // 2
    hand(middle).start()

    @pl.loop(1, middle, unroll=3)
    def _(k):
        hand(middle + k).start()
        hand(middle - k).start()

    rows_in[p] = rows_out[p]

    @pl.loop(1, size_x, unroll=unroll_x)
    def _(k):
        hand(k).wait()

    arrived = rows_in[:, :, 0 : 2 * STEP].reshape(size_x, 2 * STEP)
    column = iota((size_x, n_out), 1)
    start = lx * iota((size_x, n_out), 0)
    home = (column >= start) & (column < start + lx)
    wide_rows = dot_nn(jnp.concatenate(split3(arrived), 0), table[...])
    wide_rows = wide_rows[0:size_x] + wide_rows[size_x : 2 * size_x] + wide_rows[2 * size_x :]
    energy_out[...] = jnp.sum(jnp.where(home, wide_rows, 0.0), 0, keepdims=True)

    for u in range(len(units)):
        to_outer(u).wait_send()
        to_beyond(u).wait_send()
        to_partner(u).wait_send()
        forward(u).wait_send()
        to_left(u).wait_send()
        to_right(u).wait_send()


def per_device(background, slab_owner, class_length_scale, band_widths, x_class, y_class, z_class):
    lx, ly, nslab = background.shape
    nvar, lev = z_class.shape
    size_x = lax.axis_size("sx")
    size_y = lax.axis_size("sy")
    span = lx + 2 * REACH
    vmem = pl.BlockSpec(memory_space=pltpu.VMEM)
    energy, cov = pl.pallas_call(
        functools.partial(kernel, size_x, size_y, lev),
        out_shape=(
            pltpu.VMEM((1, size_x * lx), F32),
            pltpu.VMEM((lx, ly, nslab), BF16),
        ),
        in_specs=[pl.BlockSpec(memory_space=pl.ANY)] * 7,
        out_specs=(vmem, vmem),
        scratch_shapes=[
            pltpu.VMEM((lx, ly, LANES), BF16),
            pltpu.VMEM((lx, ly, nslab), BF16),
            pltpu.VMEM((nvar, ly // PACK, span, PACK, LANES), BF16),
            pltpu.VMEM((nvar, lx, ly + 2 * REACH, LANES), BF16),
            pltpu.VMEM((nvar, lx, ly, LANES), BF16),
            pltpu.VMEM((nvar, lx * PACK, span * PACK), BF16),
            pltpu.VMEM((nvar, ly, LANES), BF16),
            pltpu.VMEM((nvar, 2 * LANES, LANES), BF16),
            pltpu.VMEM((nvar, LANES, LANES), BF16),
            pltpu.VMEM((LANES, span * PACK), BF16),
            pltpu.VMEM((8, LANES), jnp.int32),
            pltpu.VMEM((nvar, size_y * LANES, LANES), BF16),
            pltpu.VMEM((nvar, 2 * STEP, LANES), F32),
            pltpu.VMEM((2 * STEP, size_y * LANES), F32),
            pltpu.VMEM((size_y, STEP, LANES), F32),
            pltpu.VMEM((size_y, STEP, LANES), F32),
            pltpu.VMEM((size_x, 1, LANES), F32),
            pltpu.VMEM((size_x, 1, LANES), F32),
            pltpu.VMEM((2 * STEP, size_x * lx), BF16),
            pltpu.VMEM((8, LANES), jnp.int32),
            pltpu.SemaphoreType.DMA,
            pltpu.SemaphoreType.DMA,
            pltpu.SemaphoreType.DMA((nvar + 1, 4)),
            pltpu.SemaphoreType.DMA((nvar + 1, 4)),
            pltpu.SemaphoreType.DMA((nvar + 1, 2)),
            pltpu.SemaphoreType.DMA((nvar + 1, 2)),
            pltpu.SemaphoreType.DMA((size_y,)),
            pltpu.SemaphoreType.DMA((size_y,)),
            pltpu.SemaphoreType.DMA((size_x,)),
            pltpu.SemaphoreType.DMA((size_x,)),
            pltpu.SemaphoreType.REGULAR((2, 8, 2)),
            pltpu.VMEM(slab_owner.shape, jnp.int32),
            pltpu.SMEM(class_length_scale.shape, F32),
            pltpu.SMEM(band_widths.shape, jnp.int32),
            pltpu.VMEM(x_class.shape, jnp.int32),
            pltpu.VMEM(y_class.shape, jnp.int32),
            pltpu.VMEM(z_class.shape, jnp.int32),
            pltpu.SemaphoreType.DMA((6,)),
        ],
        compiler_params=pltpu.CompilerParams(
            collective_id=0, has_side_effects=True, vmem_limit_bytes=60000 * 1024
        ),
    )(background, slab_owner, class_length_scale, band_widths, x_class, y_class, z_class)
    return energy, cov


def solution(mesh):
    in_specs = (P("sx", "sy", None), P(), P(), P(), P(), P(), P())
    out_specs = (P(("sx", "sy"), None), P("sx", "sy", None))
    return jax.shard_map(per_device, mesh=mesh, in_specs=in_specs, out_specs=out_specs, check_vma=False)
```

```python
import functools

import jax
import jax.numpy as jnp
from jax import lax
from jax.experimental import pallas as pl
from jax.experimental.pallas import tpu as pltpu
from jax.sharding import PartitionSpec as P

MESH = pl.DeviceIdType.MESH
REACH = 32
LANES = 128
PACK = 8
HALF = 12
STEP = 16
MIDDLE = 4
F32 = jnp.float32
BF16 = jnp.bfloat16


def iota(shape, dim):
    return lax.broadcasted_iota(jnp.int32, shape, dim)


def lookup(classes, table):
    out = jnp.zeros(classes.shape, table.dtype)
    for k in range(table.shape[0]):
        out = jnp.where(classes == k, table[k], out)
    return out


def bump_of(offset, inside, scale):
    ratio = offset.astype(F32) / scale
    return jnp.where(inside, jnp.exp(-0.5 * ratio * ratio), jnp.float32(0.0))


def normalised(bump):
    return bump * lax.rsqrt(jnp.sum(bump * bump, 0, keepdims=True))


def dot_nt(a, b):
    return lax.dot_general(a, b, (((1,), (1,)), ((), ())), preferred_element_type=F32)


def dot_nn(a, b):
    return jnp.dot(a, b, preferred_element_type=F32)


def split3(value):
    high = value.astype(BF16)
    rest = value - high.astype(F32)
    middle = rest.astype(BF16)
    low = (rest - middle.astype(F32)).astype(BF16)
    return high, middle, low


def kernel(
    size_x,
    size_y,
    lev,
    background,
    slab_owner_hbm,
    scale_table_hbm,
    reach_table_hbm,
    x_class_hbm,
    y_class_hbm,
    z_class_hbm,
    energy_out,
    cov_out,
    first_tile,
    raw,
    win,
    xfw,
    yr,
    kron,
    wy,
    wz,
    wxt,
    spread,
    tables,
    onehot,
    mine,
    slots,
    outbox,
    inbox,
    rows_out,
    rows_in,
    table,
    fill,
    first_sem,
    raw_sem,
    near_send,
    near_recv,
    side_send,
    side_recv,
    sum_send,
    sum_recv,
    row_send,
    row_recv,
    greeted,
    slab_owner,
    scale_table,
    reach_table,
    x_class,
    y_class,
    z_class,
    small_sem,
):
    lx, ly, nslab = background.shape
    nvar = z_class.shape[0]
    far = REACH - lx
    span = lx + 2 * REACH
    p = lax.axis_index("sx")
    q = lax.axis_index("sy")
    core = lax.rem(p, 2)
    unroll_x = 7 if size_x % 7 == 1 else 1

    def at_x(step):
        return (lax.rem(p + step + size_x, size_x), q)

    def at_y(step):
        return (p, lax.rem(q + step + size_y, size_y))

    load_first = pltpu.make_async_copy(background.at[:, :, 0:LANES], first_tile, first_sem)
    load_first.start()
    load = pltpu.make_async_copy(background, raw, raw_sem)
    load.start()
    smalls = []
    for k, (src, dst) in enumerate((
        (slab_owner_hbm, slab_owner), (scale_table_hbm, scale_table), (reach_table_hbm, reach_table),
        (x_class_hbm, x_class), (y_class_hbm, y_class), (z_class_hbm, z_class),
    )):
        smalls.append(pltpu.make_async_copy(src, dst, small_sem.at[k]))
        smalls[-1].start()
    barrier = pltpu.get_barrier_semaphore()

    near = (at_x(-2), at_x(-1), at_x(1), at_x(2), at_y(-1), at_y(1))
    for peer in near:
        pl.semaphore_signal(barrier, inc=1, device_id=peer, device_id_type=MESH)

    def doublings(known, size):
        reach = []
        while known < size // 2:
            reach.append(known)
            known *= 2
        return reach

    rounds = max(len(doublings(2, size_x)), len(doublings(1, size_y)))

    def greet(r):
        for axis, at, reach in ((0, at_x, doublings(2, size_x)), (1, at_y, doublings(1, size_y))):
            if r < len(reach):
                for side, step in ((0, reach[r]), (1, -reach[r])):
                    pl.semaphore_signal(greeted.at[axis, r, side], inc=1, device_id=at(step), device_id_type=MESH)

    def heard(r):
        for axis, reach in ((0, doublings(2, size_x)), (1, doublings(1, size_y))):
            if r < len(reach):
                for side in range(2):
                    pl.semaphore_wait(greeted.at[axis, r, side], 1)

    outer = at_x(2 * core - 1)
    partner = at_x(1 - 2 * core)
    beyond = at_x(2 - 4 * core)

    def remote(src, dst, send, recv, peer):
        return pltpu.make_async_remote_copy(
            src_ref=src, dst_ref=dst, send_sem=send, recv_sem=recv, device_id=peer, device_id_type=MESH
        )

    blocks = ly // PACK
    order = list(range((blocks - MIDDLE) // 2, (blocks + MIDDLE) // 2))
    for k in range((blocks - MIDDLE) // 2 - 1, -1, -1):
        order += [k, blocks - 1 - k]
    units = [(v, 0, blocks) for v in range(nvar - 1)]
    units += [(nvar - 1, 0, MIDDLE)] + [(nvar - 1, k, 2) for k in range(MIDDLE, blocks, 2)]

    def window(u, first, count):
        return win.at[units[u][0], pl.ds(units[u][1], units[u][2]), pl.ds(first, count)]

    def to_outer_edge(u):
        own = window(u, REACH + (lx - far) * core, far)
        return remote(own, window(u, REACH + lx - (lx + far) * core, far), near_send.at[u, 0], near_recv.at[u, 0], outer)

    def to_outer(u):
        own = window(u, REACH + far - far * core, lx - far)
        return remote(own, window(u, REACH + lx + far - (2 * lx + far) * core, lx - far), near_send.at[u, 4], near_recv.at[u, 4], outer)

    def to_partner(u):
        own = window(u, REACH, lx)
        return remote(own, window(u, far + 2 * lx * core, lx), near_send.at[u, 1], near_recv.at[u, 1], partner)

    def to_beyond(u):
        own = window(u, REACH + (lx - far) * (1 - core), far)
        return remote(own, window(u, (span - far) * core, far), near_send.at[u, 2], near_recv.at[u, 2], beyond)

    def forward(u):
        got = window(u, far + (lx - far) + REACH * core, far)
        return remote(got, window(u, (span - far) * core, far), near_send.at[u, 3], near_recv.at[u, 3], partner)

    def columns(u):
        _, first, count = units[u]
        stored = order[first : first + count]
        left = [k for k in stored if k < blocks // 2]
        right = [k - blocks // 2 for k in stored if k >= blocks // 2]
        return min(left) * PACK, min(right) * PACK, len(left) * PACK

    def to_left(u):
        v, (first, _, count) = units[u][0], columns(u)
        own = xfw.at[v, :, pl.ds(REACH + first, count)]
        return remote(own, xfw.at[v, :, pl.ds(REACH + ly + first, count)], side_send.at[u, 0], side_recv.at[u, 0], at_y(-1))

    def to_right(u):
        v, (_, first, count) = units[u][0], columns(u)
        own = xfw.at[v, :, pl.ds(ly + first, count)]
        return remote(own, xfw.at[v, :, pl.ds(first, count)], side_send.at[u, 1], side_recv.at[u, 1], at_y(1))

    def align(v):
        rows = 4
        column = iota((ly, LANES), 1)

        @pl.loop(0, lx // rows)
        def _(block):
            for r in range(rows):
                i = block * rows + r
                if LANES * (v + 1) > nslab:
                    win[v, :, REACH + i] = jnp.zeros((ly // PACK, PACK, LANES), BF16)
                    piece = raw[i, :, lev * v : lev * (v + 1)].reshape(blocks, PACK, lev)
                    for k in range(blocks):
                        win[v, k, REACH + i, :, 0:lev] = piece[order[k]]
                    continue
                tile = (first_tile[i] if v == 0 else raw[i, :, LANES * v : LANES * (v + 1)]).astype(F32)
                if v > 0:
                    before = raw[i, :, LANES * (v - 1) : LANES * v].astype(F32)
                    tile = pltpu.roll(jnp.where(column >= LANES - v, before, tile), v, 1)
                tile = jnp.where(column < lev, tile, 0.0).astype(BF16)
                tile = tile.reshape(blocks, PACK, LANES)
                for k in range(blocks):
                    win[v, k, REACH + i] = tile[order[k]]

    load_first.wait()
    align(0)
    pl.semaphore_wait(barrier, len(near))
    for u in range(len(units)):
        to_outer_edge(u).start()
        to_beyond(u).start()
        to_outer(u).start()
        to_partner(u).start()
        if u == 0:
            greet(0)
            load.wait()
            align(1)
        if u + 2 < nvar:
            align(u + 2)
    for copy in smalls:
        copy.wait()

    n_x = size_x * lx
    n_y = size_y * ly
    lane_x = iota((n_x, LANES), 1)
    pick_x = ((iota((n_x, LANES), 0) == lx * p + lane_x) & (lane_x < lx)).astype(BF16)
    cls_x = (dot_nn(x_class[...].astype(F32).astype(BF16), pick_x) + 0.5).astype(jnp.int32)
    lane_y = iota((n_y, LANES), 1)
    pick_y = ((iota((n_y, LANES), 0) == ly * q + lane_y) & (lane_y < ly)).astype(BF16)
    cls_y = (dot_nn(y_class[...].astype(F32).astype(BF16), pick_y) + 0.5).astype(jnp.int32)
    scale_x, reach_x = lookup(cls_x, scale_table), lookup(cls_x, reach_table)
    scale_y, reach_y = lookup(cls_y, scale_table), lookup(cls_y, reach_table)
    lane = iota((LANES, LANES), 1)
    depth = iota((LANES, LANES), 0)
    offset = depth - REACH - lane
    col_x = lx * p - REACH + depth
    col_y = ly * q - REACH + depth
    eye = (iota((ly, LANES), 0) == iota((ly, LANES), 1)).astype(BF16)
    for v in range(nvar):
        near = jnp.abs(offset)
        inside = (near <= reach_x[v : v + 1]) & (col_x >= 0) & (col_x < n_x) & (depth < span)
        weight = normalised(bump_of(offset, inside, scale_x[v : v + 1]))
        wxt[v] = jnp.where(lane < lx, weight, 0.0).astype(BF16)
        inside = (near <= reach_y[v : v + 1]) & (col_y >= 0) & (col_y < n_y)
        weight = normalised(bump_of(offset, inside, scale_y[v : v + 1]))
        wy[v] = dot_nt(eye, jnp.where(lane < ly, weight, 0.0).astype(BF16)).astype(BF16)

    spread[...] = (iota(spread.shape, 1) // PACK == iota(spread.shape, 0)).astype(BF16)
    part = lx * PACK // 2

    @pl.loop(0, nvar * 2)
    def _(step):
        v = step // 2
        first = pl.multiple_of((step % 2) * part, 16)
        row = iota((part, LANES), 0) + first
        pick = (row // PACK == iota((part, LANES), 1)).astype(BF16)
        rows = dot_nt(pick, wxt[v]).astype(BF16)
        wide = dot_nn(rows, spread[...])
        same = (iota(wide.shape, 0) % PACK) == (iota(wide.shape, 1) % PACK)
        kron[v, pl.ds(first, part), :] = jnp.where(same, wide, 0.0).astype(BF16)

    tables[...] = jnp.zeros(tables.shape, jnp.int32)
    tables[0:nvar, 0:lev] = z_class[...]
    lane1 = iota((8, LANES), 1)
    for t in range(nvar):
        here = pltpu.roll(tables[...], (LANES - t) % LANES, 1)[t : t + 1]
        if t + 1 < nvar:
            there = pltpu.roll(tables[...], lev - t, 1)[t + 1 : t + 2]
        else:
            there = here
        cls_z = jnp.where(lane1[0:1] < lev - t, here, there)
        scale_z, reach_z = lookup(cls_z, scale_table), lookup(cls_z, reach_table)
        own = lane < lev - t
        offset_z = depth - (lane + t)
        inside = (jnp.abs(offset_z) <= reach_z) & own & (depth < lev)
        upper = normalised(bump_of(offset_z, inside, scale_z))
        wz[t, 0:LANES] = jnp.where(own, upper, 0.0).astype(BF16)
        if t + 1 < nvar:
            offset_z = depth - (lane - (lev - t))
            inside = (jnp.abs(offset_z) <= reach_z) & (lane >= lev - t) & (depth < lev)
            lower = normalised(bump_of(offset_z, inside, scale_z))
            wz[t, LANES : 2 * LANES] = jnp.where(lane >= lev - t, lower, 0.0).astype(BF16)

    fill[...] = jnp.full(fill.shape, -1, jnp.int32)
    for v in range(nvar):
        fill[v : v + 1, 0:lev] = slab_owner[lev * v : lev * (v + 1)].reshape(1, lev)
    for v in range(nvar):
        owner = fill[v : v + 1, :]
        owner_x = (owner * ((1 << 19) // size_y + 1)) >> 19
        place = jnp.where(owner >= 0, owner_x + LANES * (owner - owner_x * size_y), -1)
        onehot[v] = (iota((size_y * LANES, LANES), 0) == place).astype(BF16)
    n_out = size_x * lx
    cell = iota(table.shape, 1) % lx
    table[...] = (cell + (STEP - HALF) * (cell // HALF) == iota(table.shape, 0)).astype(BF16)
    mine[...] = jnp.zeros(mine.shape, F32)
    rows_out[...] = jnp.zeros(rows_out.shape, F32)
    eye_x = (iota((size_x, LANES), 0) == iota((size_x, LANES), 1)).astype(BF16)

    def filter_x(u):
        v, first_block, count = units[u]
        wide = min(MIDDLE, count)
        for at in range(first_block, first_block + count, wide):
            parts = [win[v, at + k].reshape(span * PACK, LANES) for k in range(wide)]
            got = dot_nn(kron[v], jnp.concatenate(parts, 1)).reshape(lx, PACK, wide * LANES)
            for k in range(wide):
                first = order[at + k] * PACK + REACH
                xfw[v, :, first : first + PACK, :] = got[:, :, LANES * k : LANES * (k + 1)].astype(BF16)

    def filter_y(v):
        rows = HALF

        @pl.loop(0, lx // rows)
        def _(block):
            for r in range(0, rows, 2):
                i = block * rows + r
                both = jnp.concatenate([xfw[v, i], xfw[v, i + 1]], 1)
                got = dot_nn(wy[v], both)
                power = jnp.sum(got * got, 0, keepdims=True)
                for k in range(2):
                    yr[v, i + k] = got[:, LANES * k : LANES * (k + 1)].astype(BF16)
                    mine[v, pl.ds(block * STEP + r + k, 1), :] = power[:, LANES * k : LANES * (k + 1)]

    def filter_z(t):
        rows = 8
        width = min(LANES, nslab - LANES * t)

        @pl.loop(0, lx // rows)
        def _(block):
            first = block * rows
            here = yr[t, pl.ds(first, rows)].reshape(rows * ly, LANES)
            if t + 1 < nvar:
                there = yr[t + 1, pl.ds(first, rows)].reshape(rows * ly, LANES)
                got = dot_nn(jnp.concatenate([here, there], 1), wz[t])
            else:
                got = dot_nn(here, wz[t, 0:LANES])
            got = got.astype(BF16).reshape(rows, ly, LANES)
            cov_out[pl.ds(first, rows), :, LANES * t : LANES * t + width] = got[:, :, 0:width]

    def gather_slots(v):
        got = dot_nt(jnp.concatenate(split3(mine[v]), 0), onehot[v])
        rows = mine.shape[1]
        got = got[0:rows] + got[rows : 2 * rows] + got[2 * rows :]
        if v == 0:
            slots[...] = got
        else:
            slots[...] += got

    def tell(k):
        to = lax.rem(q + k, size_y)
        return remote(outbox.at[to], inbox.at[k], sum_send.at[k], sum_recv.at[k], (p, to))

    def hand(k):
        to = lax.rem(p + k, size_x)
        return remote(rows_out.at[to], rows_in.at[p], row_send.at[k], row_recv.at[k], (to, q))

    def arrive(u):
        to_outer_edge(u).wait_recv()
        forward(u).start()
        to_beyond(u).wait_recv()
        to_partner(u).wait_recv()
        forward(u).wait_recv()
        to_outer(u).wait_recv()
        filter_x(u)
        to_left(u).start()
        to_right(u).start()

    def sides(v):
        for u in range(len(units)):
            if units[u][0] == v:
                to_left(u).wait_recv()
                to_right(u).wait_recv()

    heard(0)
    greet(1)
    for u in range(nvar):
        arrive(u)
        if u + 1 < rounds:
            heard(u + 1)
            greet(u + 2)
        if u >= 1:
            sides(u - 1)
            filter_y(u - 1)
            gather_slots(u - 1)
        if 2 <= u < nvar - 1:
            filter_z(u - 2)
    v = nvar - 1
    for u in range(nvar, len(units)):
        arrive(u)
    filter_z(v - 2)
    sides(v)
    filter_y(v)
    gather_slots(v)
    for to in range(size_y):
        block = slots[:, LANES * to : LANES * (to + 1)]
        outbox[to] = block[0:STEP] + pltpu.roll(block[STEP : 2 * STEP], LANES // 2, 1)

    for k in sorted(range(1, size_y), key=lambda k: abs(2 * k - size_y)):
        tell(k).start()

    filter_z(v - 1)
    filter_z(v)

    @pl.loop(1, size_y, unroll=True)
    def _(k):
        tell(k).wait()

    total = outbox[q]
    for k in range(1, size_y):
        total = total + inbox[k]
    both = jnp.concatenate([total, pltpu.roll(total, LANES // 2, 1)], 0)
    picked = jnp.zeros((size_x, 2 * STEP), F32)
    for piece in split3(both):
        picked = picked + dot_nt(eye_x, piece)
    rows_out[:, :, 0 : 2 * STEP] = picked.reshape(size_x, 1, 2 * STEP)

    middle = size_x // 2
    hand(middle).start()

    @pl.loop(1, middle, unroll=3)
    def _(k):
        hand(middle + k).start()
        hand(middle - k).start()

    rows_in[p] = rows_out[p]

    @pl.loop(1, size_x, unroll=unroll_x)
    def _(k):
        hand(k).wait()

    arrived = rows_in[:, :, 0 : 2 * STEP].reshape(size_x, 2 * STEP)
    pieces = split3(arrived)
    for low in range(0, n_out, LANES):
        high = min(n_out, low + LANES)
        top = low // lx // 8 * 8
        end = min(size_x, -(-high // lx) + 7 - (-(-high // lx) + 7) % 8)
        column = iota((end - top, high - low), 1) + low
        start = lx * (iota((end - top, high - low), 0) + top)
        home = (column >= start) & (column < start + lx)
        got = jnp.zeros(home.shape, F32)
        for piece in pieces:
            got = got + dot_nn(piece[top:end], table[:, low:high])
        energy_out[:, low:high] = jnp.sum(jnp.where(home, got, 0.0), 0, keepdims=True)

    for u in range(len(units)):
        to_outer_edge(u).wait_send()
        to_outer(u).wait_send()
        to_beyond(u).wait_send()
        to_partner(u).wait_send()
        forward(u).wait_send()
        to_left(u).wait_send()
        to_right(u).wait_send()


def per_device(background, slab_owner, class_length_scale, band_widths, x_class, y_class, z_class):
    lx, ly, nslab = background.shape
    nvar, lev = z_class.shape
    size_x = lax.axis_size("sx")
    size_y = lax.axis_size("sy")
    span = lx + 2 * REACH
    vmem = pl.BlockSpec(memory_space=pltpu.VMEM)
    energy, cov = pl.pallas_call(
        functools.partial(kernel, size_x, size_y, lev),
        out_shape=(
            pltpu.VMEM((1, size_x * lx), F32),
            pltpu.VMEM((lx, ly, nslab), BF16),
        ),
        in_specs=[pl.BlockSpec(memory_space=pl.ANY)] * 7,
        out_specs=(vmem, vmem),
        scratch_shapes=[
            pltpu.VMEM((lx, ly, LANES), BF16),
            pltpu.VMEM((lx, ly, nslab), BF16),
            pltpu.VMEM((nvar, ly // PACK, span, PACK, LANES), BF16),
            pltpu.VMEM((nvar, lx, ly + 2 * REACH, LANES), BF16),
            pltpu.VMEM((nvar, lx, ly, LANES), BF16),
            pltpu.VMEM((nvar, lx * PACK, span * PACK), BF16),
            pltpu.VMEM((nvar, ly, LANES), BF16),
            pltpu.VMEM((nvar, 2 * LANES, LANES), BF16),
            pltpu.VMEM((nvar, LANES, LANES), BF16),
            pltpu.VMEM((LANES, span * PACK), BF16),
            pltpu.VMEM((8, LANES), jnp.int32),
            pltpu.VMEM((nvar, size_y * LANES, LANES), BF16),
            pltpu.VMEM((nvar, 2 * STEP, LANES), F32),
            pltpu.VMEM((2 * STEP, size_y * LANES), F32),
            pltpu.VMEM((size_y, STEP, LANES), F32),
            pltpu.VMEM((size_y, STEP, LANES), F32),
            pltpu.VMEM((size_x, 1, LANES), F32),
            pltpu.VMEM((size_x, 1, LANES), F32),
            pltpu.VMEM((2 * STEP, size_x * lx), BF16),
            pltpu.VMEM((8, LANES), jnp.int32),
            pltpu.SemaphoreType.DMA,
            pltpu.SemaphoreType.DMA,
            pltpu.SemaphoreType.DMA((nvar + 2, 5)),
            pltpu.SemaphoreType.DMA((nvar + 2, 5)),
            pltpu.SemaphoreType.DMA((nvar + 2, 2)),
            pltpu.SemaphoreType.DMA((nvar + 2, 2)),
            pltpu.SemaphoreType.DMA((size_y,)),
            pltpu.SemaphoreType.DMA((size_y,)),
            pltpu.SemaphoreType.DMA((size_x,)),
            pltpu.SemaphoreType.DMA((size_x,)),
            pltpu.SemaphoreType.REGULAR((2, 8, 2)),
            pltpu.VMEM(slab_owner.shape, jnp.int32),
            pltpu.SMEM(class_length_scale.shape, F32),
            pltpu.SMEM(band_widths.shape, jnp.int32),
            pltpu.VMEM(x_class.shape, jnp.int32),
            pltpu.VMEM(y_class.shape, jnp.int32),
            pltpu.VMEM(z_class.shape, jnp.int32),
            pltpu.SemaphoreType.DMA((6,)),
        ],
        compiler_params=pltpu.CompilerParams(
            collective_id=0, has_side_effects=True, vmem_limit_bytes=60000 * 1024
        ),
    )(background, slab_owner, class_length_scale, band_widths, x_class, y_class, z_class)
    return energy, cov


def solution(mesh):
    in_specs = (P("sx", "sy", None), P(), P(), P(), P(), P(), P())
    out_specs = (P(("sx", "sy"), None), P("sx", "sy", None))
    return jax.shard_map(per_device, mesh=mesh, in_specs=in_specs, out_specs=out_specs, check_vma=False)
```

```python
import functools

import jax
import jax.numpy as jnp
from jax import lax
from jax.experimental import pallas as pl
from jax.experimental.pallas import tpu as pltpu
from jax.sharding import PartitionSpec as P

MESH = pl.DeviceIdType.MESH
REACH = 32
LANES = 128
PACK = 8
HALF = 12
STEP = 16
MIDDLE = 4
F32 = jnp.float32
BF16 = jnp.bfloat16


def iota(shape, dim):
    return lax.broadcasted_iota(jnp.int32, shape, dim)


def lookup(classes, table):
    out = jnp.zeros(classes.shape, table.dtype)
    for k in range(table.shape[0]):
        out = jnp.where(classes == k, table[k], out)
    return out


def bump_of(offset, inside, scale):
    ratio = offset.astype(F32) / scale
    return jnp.where(inside, jnp.exp(-0.5 * ratio * ratio), jnp.float32(0.0))


def normalised(bump):
    return bump * lax.rsqrt(jnp.sum(bump * bump, 0, keepdims=True))


def dot_nt(a, b):
    return lax.dot_general(a, b, (((1,), (1,)), ((), ())), preferred_element_type=F32)


def dot_nn(a, b):
    return jnp.dot(a, b, preferred_element_type=F32)


def split3(value):
    high = value.astype(BF16)
    rest = value - high.astype(F32)
    middle = rest.astype(BF16)
    low = (rest - middle.astype(F32)).astype(BF16)
    return high, middle, low


def kernel(
    size_x,
    size_y,
    lev,
    background,
    slab_owner_hbm,
    scale_table_hbm,
    reach_table_hbm,
    x_class_hbm,
    y_class_hbm,
    z_class_hbm,
    energy_out,
    cov_out,
    raw,
    win,
    xfw,
    yr,
    kron,
    wy,
    wz,
    wxt,
    spread,
    tables,
    onehot,
    mine,
    slots,
    outbox,
    inbox,
    rows_out,
    rows_in,
    table,
    fill,
    first_sem,
    raw_sem,
    near_send,
    near_recv,
    side_send,
    side_recv,
    sum_send,
    sum_recv,
    row_send,
    row_recv,
    greeted,
    slab_owner,
    scale_table,
    reach_table,
    x_class,
    y_class,
    z_class,
    small_sem,
):
    lx, ly, nslab = background.shape
    nvar = z_class.shape[0]
    far = REACH - lx
    span = lx + 2 * REACH
    p = lax.axis_index("sx")
    q = lax.axis_index("sy")
    core = lax.rem(p, 2)
    unroll_x = 7 if size_x % 7 == 1 else 1

    def at_x(step):
        return (lax.rem(p + step + size_x, size_x), q)

    def at_y(step):
        return (p, lax.rem(q + step + size_y, size_y))

    blocks = ly // PACK
    order = list(range((blocks - MIDDLE) // 2, (blocks + MIDDLE) // 2))
    for k in range((blocks - MIDDLE) // 2 - 1, -1, -1):
        order += [k, blocks - 1 - k]
    firsts = []
    for k in range(blocks):
        rows = background.at[:, order[k] * PACK : (order[k] + 1) * PACK, 0:LANES]
        firsts.append(pltpu.make_async_copy(rows, win.at[0, k, REACH : REACH + lx], first_sem.at[k]))
        firsts[-1].start()
    load = pltpu.make_async_copy(background, raw, raw_sem)
    load.start()
    smalls = []
    for k, (src, dst) in enumerate((
        (slab_owner_hbm, slab_owner), (scale_table_hbm, scale_table), (reach_table_hbm, reach_table),
        (x_class_hbm, x_class), (y_class_hbm, y_class), (z_class_hbm, z_class),
    )):
        smalls.append(pltpu.make_async_copy(src, dst, small_sem.at[k]))
        smalls[-1].start()
    barrier = pltpu.get_barrier_semaphore()

    near = (at_x(-2), at_x(-1), at_x(1), at_x(2), at_y(-1), at_y(1))
    for peer in near:
        pl.semaphore_signal(barrier, inc=1, device_id=peer, device_id_type=MESH)

    def doublings(known, size):
        reach = []
        while known < size // 2:
            reach.append(known)
            known *= 2
        return reach

    rounds = max(len(doublings(2, size_x)), len(doublings(1, size_y)))

    def greet(r):
        for axis, at, reach in ((0, at_x, doublings(2, size_x)), (1, at_y, doublings(1, size_y))):
            if r < len(reach):
                for side, step in ((0, reach[r]), (1, -reach[r])):
                    pl.semaphore_signal(greeted.at[axis, r, side], inc=1, device_id=at(step), device_id_type=MESH)

    def heard(r):
        for axis, reach in ((0, doublings(2, size_x)), (1, doublings(1, size_y))):
            if r < len(reach):
                for side in range(2):
                    pl.semaphore_wait(greeted.at[axis, r, side], 1)

    outer = at_x(2 * core - 1)
    partner = at_x(1 - 2 * core)
    beyond = at_x(2 - 4 * core)

    def remote(src, dst, send, recv, peer):
        return pltpu.make_async_remote_copy(
            src_ref=src, dst_ref=dst, send_sem=send, recv_sem=recv, device_id=peer, device_id_type=MESH
        )

    units = [(v, 0, blocks) for v in range(nvar - 1)]
    units += [(nvar - 1, 0, MIDDLE)] + [(nvar - 1, k, 2) for k in range(MIDDLE, blocks, 2)]

    def window(u, first, count):
        return win.at[units[u][0], pl.ds(units[u][1], units[u][2]), pl.ds(first, count)]

    def to_outer_edge(u):
        own = window(u, REACH + (lx - far) * core, far)
        return remote(own, window(u, REACH + lx - (lx + far) * core, far), near_send.at[u, 0], near_recv.at[u, 0], outer)

    def to_outer(u):
        own = window(u, REACH + far - far * core, lx - far)
        return remote(own, window(u, REACH + lx + far - (2 * lx + far) * core, lx - far), near_send.at[u, 4], near_recv.at[u, 4], outer)

    def to_partner(u):
        own = window(u, REACH, lx)
        return remote(own, window(u, far + 2 * lx * core, lx), near_send.at[u, 1], near_recv.at[u, 1], partner)

    def to_beyond(u):
        own = window(u, REACH + (lx - far) * (1 - core), far)
        return remote(own, window(u, (span - far) * core, far), near_send.at[u, 2], near_recv.at[u, 2], beyond)

    def forward(u):
        got = window(u, far + (lx - far) + REACH * core, far)
        return remote(got, window(u, (span - far) * core, far), near_send.at[u, 3], near_recv.at[u, 3], partner)

    def columns(u):
        _, first, count = units[u]
        stored = order[first : first + count]
        left = [k for k in stored if k < blocks // 2]
        right = [k - blocks // 2 for k in stored if k >= blocks // 2]
        return min(left) * PACK, min(right) * PACK, len(left) * PACK

    def to_left(u):
        v, (first, _, count) = units[u][0], columns(u)
        own = xfw.at[v, :, pl.ds(REACH + first, count)]
        return remote(own, xfw.at[v, :, pl.ds(REACH + ly + first, count)], side_send.at[u, 0], side_recv.at[u, 0], at_y(-1))

    def to_right(u):
        v, (_, first, count) = units[u][0], columns(u)
        own = xfw.at[v, :, pl.ds(ly + first, count)]
        return remote(own, xfw.at[v, :, pl.ds(first, count)], side_send.at[u, 1], side_recv.at[u, 1], at_y(1))

    def align(v):
        rows = 4
        column = iota((ly, LANES), 1)

        @pl.loop(0, lx // rows)
        def _(block):
            for r in range(rows):
                i = block * rows + r
                if LANES * (v + 1) > nslab:
                    win[v, :, REACH + i] = jnp.zeros((ly // PACK, PACK, LANES), BF16)
                    piece = raw[i, :, lev * v : lev * (v + 1)].reshape(blocks, PACK, lev)
                    for k in range(blocks):
                        win[v, k, REACH + i, :, 0:lev] = piece[order[k]]
                    continue
                tile = raw[i, :, LANES * v : LANES * (v + 1)].astype(F32)
                before = raw[i, :, LANES * (v - 1) : LANES * v].astype(F32)
                tile = pltpu.roll(jnp.where(column >= LANES - v, before, tile), v, 1)
                tile = jnp.where(column < lev, tile, 0.0).astype(BF16)
                tile = tile.reshape(blocks, PACK, LANES)
                for k in range(blocks):
                    win[v, k, REACH + i] = tile[order[k]]

    for copy in firsts:
        copy.wait()
    pl.semaphore_wait(barrier, len(near))
    for u in range(len(units)):
        to_outer_edge(u).start()
        to_beyond(u).start()
        to_outer(u).start()
        to_partner(u).start()
        if u == 0:
            greet(0)
            load.wait()
            align(1)
        if u + 2 < nvar:
            align(u + 2)
    for copy in smalls:
        copy.wait()

    n_x = size_x * lx
    n_y = size_y * ly
    lane_x = iota((n_x, LANES), 1)
    pick_x = ((iota((n_x, LANES), 0) == lx * p + lane_x) & (lane_x < lx)).astype(BF16)
    cls_x = (dot_nn(x_class[...].astype(F32).astype(BF16), pick_x) + 0.5).astype(jnp.int32)
    lane_y = iota((n_y, LANES), 1)
    pick_y = ((iota((n_y, LANES), 0) == ly * q + lane_y) & (lane_y < ly)).astype(BF16)
    cls_y = (dot_nn(y_class[...].astype(F32).astype(BF16), pick_y) + 0.5).astype(jnp.int32)
    scale_x, reach_x = lookup(cls_x, scale_table), lookup(cls_x, reach_table)
    scale_y, reach_y = lookup(cls_y, scale_table), lookup(cls_y, reach_table)
    lane = iota((LANES, LANES), 1)
    depth = iota((LANES, LANES), 0)
    offset = depth - REACH - lane
    col_x = lx * p - REACH + depth
    col_y = ly * q - REACH + depth
    eye = (iota((ly, LANES), 0) == iota((ly, LANES), 1)).astype(BF16)
    for v in range(nvar):
        near = jnp.abs(offset)
        inside = (near <= reach_x[v : v + 1]) & (col_x >= 0) & (col_x < n_x) & (depth < span)
        weight = normalised(bump_of(offset, inside, scale_x[v : v + 1]))
        wxt[v] = jnp.where(lane < lx, weight, 0.0).astype(BF16)
        inside = (near <= reach_y[v : v + 1]) & (col_y >= 0) & (col_y < n_y)
        weight = normalised(bump_of(offset, inside, scale_y[v : v + 1]))
        wy[v] = dot_nt(eye, jnp.where(lane < ly, weight, 0.0).astype(BF16)).astype(BF16)

    spread[...] = (iota(spread.shape, 1) // PACK == iota(spread.shape, 0)).astype(BF16)
    part = lx * PACK // 2

    @pl.loop(0, nvar * 2)
    def _(step):
        v = step // 2
        first = pl.multiple_of((step % 2) * part, 16)
        row = iota((part, LANES), 0) + first
        pick = (row // PACK == iota((part, LANES), 1)).astype(BF16)
        rows = dot_nt(pick, wxt[v]).astype(BF16)
        wide = dot_nn(rows, spread[...])
        same = (iota(wide.shape, 0) % PACK) == (iota(wide.shape, 1) % PACK)
        kron[v, pl.ds(first, part), :] = jnp.where(same, wide, 0.0).astype(BF16)

    tables[...] = jnp.zeros(tables.shape, jnp.int32)
    tables[0:nvar, 0:lev] = z_class[...]
    lane1 = iota((8, LANES), 1)
    for t in range(nvar):
        here = pltpu.roll(tables[...], (LANES - t) % LANES, 1)[t : t + 1]
        if t + 1 < nvar:
            there = pltpu.roll(tables[...], lev - t, 1)[t + 1 : t + 2]
        else:
            there = here
        cls_z = jnp.where(lane1[0:1] < lev - t, here, there)
        scale_z, reach_z = lookup(cls_z, scale_table), lookup(cls_z, reach_table)
        own = lane < lev - t
        offset_z = depth - (lane + t)
        inside = (jnp.abs(offset_z) <= reach_z) & own & (depth < lev)
        upper = normalised(bump_of(offset_z, inside, scale_z))
        wz[t, 0:LANES] = jnp.where(own, upper, 0.0).astype(BF16)
        if t + 1 < nvar:
            offset_z = depth - (lane - (lev - t))
            inside = (jnp.abs(offset_z) <= reach_z) & (lane >= lev - t) & (depth < lev)
            lower = normalised(bump_of(offset_z, inside, scale_z))
            wz[t, LANES : 2 * LANES] = jnp.where(lane >= lev - t, lower, 0.0).astype(BF16)

    fill[...] = jnp.full(fill.shape, -1, jnp.int32)
    for v in range(nvar):
        fill[v : v + 1, 0:lev] = slab_owner[lev * v : lev * (v + 1)].reshape(1, lev)
    for v in range(nvar):
        owner = fill[v : v + 1, :]
        owner_x = (owner * ((1 << 19) // size_y + 1)) >> 19
        place = jnp.where(owner >= 0, owner_x + LANES * (owner - owner_x * size_y), -1)
        onehot[v] = (iota((size_y * LANES, LANES), 0) == place).astype(BF16)
    n_out = size_x * lx
    cell = iota(table.shape, 1) % lx
    table[...] = (cell + (STEP - HALF) * (cell // HALF) == iota(table.shape, 0)).astype(BF16)
    mine[...] = jnp.zeros(mine.shape, F32)
    rows_out[...] = jnp.zeros(rows_out.shape, F32)
    eye_x = (iota((size_x, LANES), 0) == iota((size_x, LANES), 1)).astype(BF16)

    def filter_x(u):
        v, first_block, count = units[u]
        wide = min(MIDDLE, count)
        for at in range(first_block, first_block + count, wide):
            parts = [win[v, at + k].reshape(span * PACK, LANES) for k in range(wide)]
            got = dot_nn(kron[v], jnp.concatenate(parts, 1)).reshape(lx, PACK, wide * LANES)
            for k in range(wide):
                first = order[at + k] * PACK + REACH
                xfw[v, :, first : first + PACK, :] = got[:, :, LANES * k : LANES * (k + 1)].astype(BF16)

    def filter_y(v):
        rows = HALF

        @pl.loop(0, lx // rows)
        def _(block):
            for r in range(0, rows, 2):
                i = block * rows + r
                both = jnp.concatenate([xfw[v, i], xfw[v, i + 1]], 1)
                got = dot_nn(wy[v], both)
                power = jnp.sum(got * got, 0, keepdims=True)
                for k in range(2):
                    yr[v, i + k] = got[:, LANES * k : LANES * (k + 1)].astype(BF16)
                    mine[v, pl.ds(block * STEP + r + k, 1), :] = power[:, LANES * k : LANES * (k + 1)]

    def filter_z(t):
        rows = 8
        width = min(LANES, nslab - LANES * t)

        @pl.loop(0, lx // rows)
        def _(block):
            first = block * rows
            here = yr[t, pl.ds(first, rows)].reshape(rows * ly, LANES)
            if t + 1 < nvar:
                there = yr[t + 1, pl.ds(first, rows)].reshape(rows * ly, LANES)
                got = dot_nn(jnp.concatenate([here, there], 1), wz[t])
            else:
                got = dot_nn(here, wz[t, 0:LANES])
            got = got.astype(BF16).reshape(rows, ly, LANES)
            cov_out[pl.ds(first, rows), :, LANES * t : LANES * t + width] = got[:, :, 0:width]

    def gather_slots(v):
        got = dot_nt(jnp.concatenate(split3(mine[v]), 0), onehot[v])
        rows = mine.shape[1]
        got = got[0:rows] + got[rows : 2 * rows] + got[2 * rows :]
        if v == 0:
            slots[...] = got
        else:
            slots[...] += got

    def tell(k):
        to = lax.rem(q + k, size_y)
        return remote(outbox.at[to], inbox.at[k], sum_send.at[k], sum_recv.at[k], (p, to))

    def hand(k):
        to = lax.rem(p + k, size_x)
        return remote(rows_out.at[to], rows_in.at[p], row_send.at[k], row_recv.at[k], (to, q))

    def arrive(u):
        to_outer_edge(u).wait_recv()
        forward(u).start()
        to_beyond(u).wait_recv()
        to_partner(u).wait_recv()
        forward(u).wait_recv()
        to_outer(u).wait_recv()
        filter_x(u)
        to_left(u).start()
        to_right(u).start()

    def sides(v):
        for u in range(len(units)):
            if units[u][0] == v:
                to_left(u).wait_recv()
                to_right(u).wait_recv()

    heard(0)
    greet(1)
    for u in range(nvar):
        arrive(u)
        if u + 1 < rounds:
            heard(u + 1)
            greet(u + 2)
        if u >= 1:
            sides(u - 1)
            filter_y(u - 1)
            gather_slots(u - 1)
        if 2 <= u < nvar - 1:
            filter_z(u - 2)
    v = nvar - 1
    for u in range(nvar, len(units)):
        arrive(u)
    filter_z(v - 2)
    sides(v)
    filter_y(v)
    gather_slots(v)
    for to in range(size_y):
        block = slots[:, LANES * to : LANES * (to + 1)]
        outbox[to] = (block[0:STEP] + pltpu.roll(block[STEP : 2 * STEP], LANES // 2, 1)).astype(BF16)

    for k in sorted(range(1, size_y), key=lambda k: abs(2 * k - size_y)):
        tell(k).start()

    filter_z(v - 1)
    filter_z(v)

    @pl.loop(1, size_y, unroll=True)
    def _(k):
        tell(k).wait()

    total = outbox[q].astype(F32)
    for k in range(1, size_y):
        total = total + inbox[k].astype(F32)
    both = jnp.concatenate([total, pltpu.roll(total, LANES // 2, 1)], 0)
    picked = jnp.zeros((size_x, 2 * STEP), F32)
    for piece in split3(both):
        picked = picked + dot_nt(eye_x, piece)
    rows_out[:, :, 0 : 2 * STEP] = picked.reshape(size_x, 1, 2 * STEP)

    middle = size_x // 2
    hand(middle).start()

    @pl.loop(1, middle, unroll=3)
    def _(k):
        hand(middle + k).start()
        hand(middle - k).start()

    rows_in[p] = rows_out[p]

    @pl.loop(1, size_x, unroll=unroll_x)
    def _(k):
        hand(k).wait()

    arrived = rows_in[:, :, 0 : 2 * STEP].reshape(size_x, 2 * STEP)
    pieces = split3(arrived)
    for low in range(0, n_out, LANES):
        high = min(n_out, low + LANES)
        top = low // lx // 8 * 8
        end = min(size_x, -(-high // lx) + 7 - (-(-high // lx) + 7) % 8)
        column = iota((end - top, high - low), 1) + low
        start = lx * (iota((end - top, high - low), 0) + top)
        home = (column >= start) & (column < start + lx)
        got = jnp.zeros(home.shape, F32)
        for piece in pieces:
            got = got + dot_nn(piece[top:end], table[:, low:high])
        energy_out[:, low:high] = jnp.sum(jnp.where(home, got, 0.0), 0, keepdims=True)

    for u in range(len(units)):
        to_outer_edge(u).wait_send()
        to_outer(u).wait_send()
        to_beyond(u).wait_send()
        to_partner(u).wait_send()
        forward(u).wait_send()
        to_left(u).wait_send()
        to_right(u).wait_send()


def per_device(background, slab_owner, class_length_scale, band_widths, x_class, y_class, z_class):
    lx, ly, nslab = background.shape
    nvar, lev = z_class.shape
    size_x = lax.axis_size("sx")
    size_y = lax.axis_size("sy")
    span = lx + 2 * REACH
    vmem = pl.BlockSpec(memory_space=pltpu.VMEM)
    energy, cov = pl.pallas_call(
        functools.partial(kernel, size_x, size_y, lev),
        out_shape=(
            pltpu.VMEM((1, size_x * lx), F32),
            pltpu.VMEM((lx, ly, nslab), BF16),
        ),
        in_specs=[pl.BlockSpec(memory_space=pl.ANY)] * 7,
        out_specs=(vmem, vmem),
        scratch_shapes=[
            pltpu.VMEM((lx, ly, nslab), BF16),
            pltpu.VMEM((nvar, ly // PACK, span, PACK, LANES), BF16),
            pltpu.VMEM((nvar, lx, ly + 2 * REACH, LANES), BF16),
            pltpu.VMEM((nvar, lx, ly, LANES), BF16),
            pltpu.VMEM((nvar, lx * PACK, span * PACK), BF16),
            pltpu.VMEM((nvar, ly, LANES), BF16),
            pltpu.VMEM((nvar, 2 * LANES, LANES), BF16),
            pltpu.VMEM((nvar, LANES, LANES), BF16),
            pltpu.VMEM((LANES, span * PACK), BF16),
            pltpu.VMEM((8, LANES), jnp.int32),
            pltpu.VMEM((nvar, size_y * LANES, LANES), BF16),
            pltpu.VMEM((nvar, 2 * STEP, LANES), F32),
            pltpu.VMEM((2 * STEP, size_y * LANES), F32),
            pltpu.VMEM((size_y, STEP, LANES), BF16),
            pltpu.VMEM((size_y, STEP, LANES), BF16),
            pltpu.VMEM((size_x, 1, LANES), F32),
            pltpu.VMEM((size_x, 1, LANES), F32),
            pltpu.VMEM((2 * STEP, size_x * lx), BF16),
            pltpu.VMEM((8, LANES), jnp.int32),
            pltpu.SemaphoreType.DMA((ly // PACK,)),
            pltpu.SemaphoreType.DMA,
            pltpu.SemaphoreType.DMA((nvar + 2, 5)),
            pltpu.SemaphoreType.DMA((nvar + 2, 5)),
            pltpu.SemaphoreType.DMA((nvar + 2, 2)),
            pltpu.SemaphoreType.DMA((nvar + 2, 2)),
            pltpu.SemaphoreType.DMA((size_y,)),
            pltpu.SemaphoreType.DMA((size_y,)),
            pltpu.SemaphoreType.DMA((size_x,)),
            pltpu.SemaphoreType.DMA((size_x,)),
            pltpu.SemaphoreType.REGULAR((2, 8, 2)),
            pltpu.VMEM(slab_owner.shape, jnp.int32),
            pltpu.SMEM(class_length_scale.shape, F32),
            pltpu.SMEM(band_widths.shape, jnp.int32),
            pltpu.VMEM(x_class.shape, jnp.int32),
            pltpu.VMEM(y_class.shape, jnp.int32),
            pltpu.VMEM(z_class.shape, jnp.int32),
            pltpu.SemaphoreType.DMA((6,)),
        ],
        compiler_params=pltpu.CompilerParams(
            collective_id=0, has_side_effects=True, vmem_limit_bytes=60000 * 1024
        ),
    )(background, slab_owner, class_length_scale, band_widths, x_class, y_class, z_class)
    return energy, cov


def solution(mesh):
    in_specs = (P("sx", "sy", None), P(), P(), P(), P(), P(), P())
    out_specs = (P(("sx", "sy"), None), P("sx", "sy", None))
    return jax.shard_map(per_device, mesh=mesh, in_specs=in_specs, out_specs=out_specs, check_vma=False)
```
